32 devices in a mesh: shot: 4 (over x, core), rcv: 8 (over z, y).
Axes of the slice: x: 2, y: 2, z: 4, core: 2. Of those that a mesh axis runs over, the one named last changes fastest.
Arguments:
- response: bfloat16 [128, 128, 64], P('shot', 'rcv'), may hold values from -0.0625 to 0.0625
- traces: bfloat16 [128, 64, 512], P('shot', 'rcv'), may hold values from -6 to 6
Outputs:
- multiples: bfloat16 [128, 64, 512], P('shot', 'rcv')
The draws below stay inside these ranges and needn't reach their ends.
All inputs are finite; a program needn't handle non-finite values.
Results may differ from the reference program's by a relative error of at most 0.001.
Values may be sent and summed in bfloat16 or wider, within the bound.
A program may use at most 256 MiB of HBM per device.

```python
import jax
import jax.numpy as jnp
from jax import lax

POSITIONS = 128
TAPS = 64
SAMPLES = 512
SHOTS = 128
RECEIVERS = 64


def block_scale(stream_key, dims, pieces, least, top_value):
    loudness = 1.0
    for dim, blocks in pieces:
        draws = jax.random.uniform(jax.random.fold_in(jax.random.fold_in(stream_key, 6), dim), (blocks,), jnp.float32, least / len(pieces), top_value / len(pieces))
        loudness = loudness * jnp.repeat(jnp.exp(draws), dims[dim] // blocks).reshape((-1,) + (1,) * (len(dims) - 1 - dim))
    return loudness


def centred(key, extent, scale, bound, cuts=(), kind=jnp.bfloat16):
    array = jax.random.normal(key, extent, jnp.float32) * scale
    if len(cuts) > 0:
        array = block_scale(key, extent, cuts, -0.22, 0.18) * array
    return jnp.clip(array, min=-bound, max=bound).astype(kind)


def setup_inputs(seed: int = 0) -> dict:
    key_list = jax.random.split(jax.random.key(seed), 3)
    return {
        "response": centred(key_list[0], (SHOTS, POSITIONS, TAPS), (POSITIONS * TAPS) ** -0.5, 0.0625, ((0, 4), (1, 8))),
        "traces": centred(key_list[1], (POSITIONS, RECEIVERS, SAMPLES), 1.0, 6.0, ((0, 4), (1, 8))),
    }


def reference(response, traces):
    padded = jnp.pad(traces, ((0, 0), (0, 0), (TAPS, 0)))
    flat_size = RECEIVERS * SAMPLES

    def add_tap(tap_index, running):
        lag = jnp.asarray(tap_index).astype(jnp.int32)
        shifted = lax.dynamic_slice_in_dim(padded, (TAPS - lag).astype(jnp.int32), SAMPLES, 2)
        column = lax.dynamic_slice_in_dim(response, lag, 1, 2)[:, :, 0]
        return running + jnp.dot(column, shifted.reshape(POSITIONS, flat_size), preferred_element_type=jnp.float32)

    running = lax.fori_loop(0, TAPS, add_tap, jnp.zeros((SHOTS, flat_size), jnp.float32))
    return running.reshape(SHOTS, RECEIVERS, SAMPLES).astype(jnp.bfloat16)
```

```python
import functools

import jax
import jax.numpy as jnp
from jax import lax
from jax.experimental import pallas as pl
from jax.experimental.pallas import tpu as pltpu
from jax.sharding import PartitionSpec as P

MESH = pl.DeviceIdType.MESH
LANES = 128
WIDTH = 256


def put(ref, value):
    for t in range(value.shape[1] // LANES):
        ref[t] = value[:, t * LANES : (t + 1) * LANES]


def put_rows(ref, start, count, stride, value):
    for t in range(value.shape[1] // LANES):
        ref[t, pl.ds(start, count, stride=stride), :] = value[:, t * LANES : (t + 1) * LANES]


def get(ref):
    return jnp.concatenate([ref[t] for t in range(ref.shape[0])], axis=1)


def get_rows(ref, start, count, stride):
    return jnp.concatenate(
        [ref[t, pl.ds(start, count, stride=stride), :] for t in range(ref.shape[0])], axis=1
    )


def turn_response(response, b_ref, y_ref, h_ref):
    shots, rows_e, taps = response.shape
    per_tile = LANES // shots
    tiles = taps // per_tile
    b_ref[:, :taps] = response.astype(jnp.float32).reshape(shots * rows_e, taps)
    stacked = jnp.concatenate(
        [b_ref[pl.ds(k, shots, stride=rows_e), :] for k in range(rows_e)], axis=0
    )
    put(y_ref, stacked.T[:taps])
    by_tap = [get_rows(y_ref, m, tiles, per_tile) for m in range(per_tile)]
    for k in range(rows_e):
        h_ref[pl.ds(k, tiles, stride=rows_e), :] = jnp.concatenate(
            [v[:, k * shots : (k + 1) * shots] for v in by_tap], axis=1
        )
    return h_ref[...].astype(jnp.bfloat16)


def turn_traces(traces, phases, a_ref, z_ref, w_ref):
    rows_d, rcv, samples = traces.shape
    blocks = samples // phases
    put(a_ref, traces.astype(jnp.float32).reshape(rows_d * rcv, samples))
    stacked = jnp.concatenate([get_rows(a_ref, r, rows_d, rcv) for r in range(rcv)], axis=0)
    put(z_ref, stacked.T)
    by_phase = [get_rows(z_ref, v, blocks, phases) for v in range(phases)]
    for r in range(rcv):
        row = jnp.concatenate([z[:, r * rows_d : (r + 1) * rows_d] for z in by_phase], axis=1)
        put_rows(w_ref, r, blocks, rcv, row)
    return get(w_ref).astype(jnp.bfloat16)


def arrange(y_ref, o_ref, acc, z_ref, f_ref):
    shots, rcv, samples = o_ref.shape
    phases = WIDTH // shots
    blocks = samples // phases
    put(acc, y_ref[...].astype(jnp.float32))
    by_rcv = [get_rows(acc, r, blocks, rcv) for r in range(rcv)]
    for u in range(phases):
        row = jnp.concatenate([v[:, u * shots : (u + 1) * shots] for v in by_rcv], axis=1)
        put_rows(z_ref, u, blocks, phases, row)
    turned = get(z_ref).T
    for r in range(rcv):
        put_rows(f_ref, r, shots, rcv, turned[r * shots : (r + 1) * shots])
    o_ref[...] = get(f_ref).reshape(shots, rcv, samples).astype(jnp.bfloat16)


def predict(
    n_shot, n_rcv, chunks,
    response_hbm, traces_hbm, o_ref,
    response_ref, traces_ref, b_ref, y_ref, h_ref, a_ref, z_ref, w_ref,
    x_ref, g_ref, xland, gland, bands, even, odd, acc,
    load, xsend, xrecv, xfwd, gsend, grecv, gfwd,
):
    shots, rows_e, taps = response_ref.shape
    rows_d, rcv, samples = traces_ref.shape
    rows, width = x_ref.shape
    phases = WIDTH // shots
    per_tile = LANES // shots
    tiles = taps // per_tile
    pad = phases // per_tile
    history = taps // phases
    ratio = rows_d // rows_e
    head = history * rcv
    half = rows // 2
    outer_d, outer_e = n_shot // 2, n_rcv // 2
    me_d, me_e = lax.axis_index("shot"), lax.axis_index("rcv")
    in_d, in_e = lax.rem(me_d, 2), lax.rem(me_e, 2)
    out_d, out_e = me_d // 2, me_e // 2
    mate_d = out_d * 2 + 1 - in_d
    mate_e = out_e * 2 + 1 - in_e

    def at_d(step):
        return lax.rem(out_d + step + outer_d, outer_d) * 2 + in_d

    def at_e(step):
        return lax.rem(out_e + step + outer_e, outer_e) * 2 + in_e

    barrier = pltpu.get_barrier_semaphore()
    peers = [(mate_d, me_e), (me_d, mate_e)]
    peers += [(at_d(i), me_e) for i in range(1, outer_d)]
    peers += [(me_d, at_e(i)) for i in range(1, outer_e)]
    for peer in peers:
        pl.semaphore_signal(barrier, inc=1, device_id=peer, device_id_type=MESH)
    fetch_r = pltpu.make_async_copy(response_hbm, response_ref, load.at[0])
    fetch_t = pltpu.make_async_copy(traces_hbm, traces_ref, load.at[1])
    fetch_r.start()
    fetch_t.start()

    part = rows // chunks

    def xcopy(src, owner, c, send, peer):
        piece = pl.ds(c * part, part)
        return pltpu.make_async_remote_copy(
            src_ref=src.at[piece],
            dst_ref=xland.at[owner, piece],
            send_sem=send,
            recv_sem=xrecv.at[owner, c],
            device_id=peer,
            device_id_type=MESH,
        )

    def gcopy(src, owner, send, peer):
        return pltpu.make_async_remote_copy(
            src_ref=src,
            dst_ref=gland.at[owner],
            send_sem=send,
            recv_sem=grecv.at[owner],
            device_id=peer,
            device_id_type=MESH,
        )

    pending = []

    def go(copy):
        copy.start()
        pending.append(copy)

    fetch_r.wait()
    g_ref[...] = turn_response(response_ref[...], b_ref, y_ref, h_ref)
    pl.semaphore_wait(barrier, len(peers))
    order = sorted(range(1, outer_e), key=lambda i: abs(2 * i - outer_e))
    for i in order:
        go(gcopy(g_ref, me_e, gsend.at[i], (me_d, at_e(i))))
    go(gcopy(g_ref, me_e, gsend.at[0], (me_d, mate_e)))
    fetch_t.wait()
    span = samples // chunks
    for c in range(chunks + 1):
        if c < chunks:
            x_ref[pl.ds(c * part, part), :] = turn_traces(
                traces_ref[:, :, pl.ds(c * span, span)], phases, a_ref, z_ref, w_ref
            )
        if c > 0:
            for i in range(1, outer_d):
                go(xcopy(x_ref, me_d, c - 1, xsend.at[i, c - 1], (at_d(i), me_e)))
    for c in range(chunks):
        go(xcopy(x_ref, me_d, c, xsend.at[0, c], (mate_d, me_e)))

    blank = jnp.zeros((rows_e, LANES), jnp.bfloat16)

    def build(e, held):
        padded = [blank] * pad
        padded += [held[a * rows_e : (a + 1) * rows_e] for a in range(tiles)]
        padded += [blank] * (pad + 1)
        for a in range(tiles + 2 * pad):
            for q in range(per_tile):
                value = padded[a]
                if q > 0:
                    value = jnp.concatenate(
                        [padded[a][:, q * shots :], padded[a + 1][:, : q * shots]], axis=1
                    )
                bands[e, q, a] = value

    def place(owner, held, h):
        even[owner, pl.ds(head + h * half, half), :] = held
        odd[owner, pl.ds(head - rcv + h * half, half), :] = held

    def add(owner, h, first=False, last=False):
        left, right = [], []
        for v1 in range(history + 1):
            if v1 % 2 == 0:
                left.append(even[owner, pl.ds(h * half + v1 * rcv, half), :])
            else:
                left.append(odd[owner, pl.ds(h * half + (v1 - 1) * rcv, half), :])
            for v0 in range(phases):
                start = taps - v1 * phases - v0 + phases
                a, q = start // per_tile, start % per_tile
                for k in range(ratio):
                    e = owner * ratio + k
                    right.append(
                        jnp.concatenate([bands[e, q, a + n] for n in range(pad)], axis=1)
                    )
        total = jnp.dot(
            jnp.concatenate(left, axis=1),
            jnp.concatenate(right, axis=0),
            preferred_element_type=jnp.float32,
        )
        mine = pl.ds(h * half, half)
        if not first:
            total = acc[mine, :] + total
        if last:
            o_ref[mine, :] = total.astype(jnp.bfloat16)
        else:
            acc[mine, :] = total

    def forward_x(i, c):
        owner = at_d(-i)
        copy = xcopy(xland.at[owner], owner, c, xfwd.at[i, c], (mate_d, me_e))
        copy.wait_recv()
        go(copy)

    for d in range(n_shot):
        even[d, pl.ds(0, head), :] = jnp.zeros((head, width), jnp.bfloat16)
        odd[d, pl.ds(0, head), :] = jnp.zeros((head, width), jnp.bfloat16)
    for h in range(2):
        place(me_d, x_ref[pl.ds(h * half, half), :], h)
    build(me_e, g_ref[...])

    def arrived(owner):
        for c in range(chunks):
            xcopy(x_ref, owner, c, xsend.at[0, c], (mate_d, me_e)).wait_recv()

    def bring(owner):
        for h in range(2):
            place(owner, xland[owner, pl.ds(h * half, half), :], h)

    todo = [(i, c) for c in range(chunks) for i in range(1, outer_d)]
    for n in range(max(outer_e - 1, len(todo))):
        if n < len(todo):
            forward_x(*todo[n])
        if n < outer_e - 1:
            owner = at_e(-order[n])
            copy = gcopy(gland.at[owner], owner, gfwd.at[n], (me_d, mate_e))
            copy.wait_recv()
            go(copy)
        if n < outer_e - 1:
            build(owner, gland[owner])
    def meet(group):
        owner = group * 2 + 1 - in_e
        gcopy(g_ref, owner, gsend.at[0], (me_d, mate_e)).wait_recv()
        build(owner, gland[owner])

    meet(out_e)
    arrived(mate_d)
    bring(mate_d)
    for i in range(1, outer_d):
        bring(at_d(-i))
    for i in range(1, outer_d):
        owner = lax.rem(out_d - i + outer_d, outer_d) * 2 + 1 - in_d
        arrived(owner)
        bring(owner)

    for n, i in enumerate([0] + order):
        group = lax.rem(out_e - i + outer_e, outer_e)
        if n > 0:
            meet(group)
        if ratio == 2:
            for h in range(2):
                add(group, h, first=n == 0, last=n == outer_e - 1)
    if ratio != 2:
        for d in range(n_shot):
            for h in range(2):
                add(d, h, first=d == 0, last=d == n_shot - 1)
    for copy in pending:
        copy.wait_send()


def shards_general(n_shot, n_rcv, response, traces):
    shots, rows_e, taps = response.shape
    rows_d, rcv, samples = traces.shape
    phases = WIDTH // shots
    blocks = samples // phases
    per_tile = LANES // shots
    tiles = taps // per_tile
    pad = phases // per_tile
    rows = blocks * rcv
    width = phases * rows_d
    chunks = 4
    f32, bf16 = jnp.float32, jnp.bfloat16

    def tiled(height, across):
        return pltpu.VMEM((across // LANES, height, LANES), f32)

    vmem = pl.BlockSpec(memory_space=pltpu.VMEM)
    outer_d, outer_e = n_shot // 2, n_rcv // 2
    head = taps // phases * rcv
    dma = pltpu.SemaphoreType.DMA
    y = pl.pallas_call(
        functools.partial(predict, n_shot, n_rcv, chunks),
        out_shape=jax.ShapeDtypeStruct((rows, WIDTH), bf16),
        in_specs=[pl.BlockSpec(memory_space=pl.ANY)] * 2,
        out_specs=vmem,
        scratch_shapes=[
            pltpu.VMEM(response.shape, bf16),
            pltpu.VMEM(traces.shape, bf16),
            pltpu.VMEM((shots * rows_e, LANES), f32),
            tiled(taps, rows_e * shots),
            pltpu.VMEM((tiles * rows_e, LANES), f32),
            tiled(rows_d * rcv, samples // chunks),
            tiled(samples // chunks, rcv * rows_d),
            tiled(rows // chunks, width),
            pltpu.VMEM((rows, width), bf16),
            pltpu.VMEM((tiles * rows_e, LANES), bf16),
            pltpu.VMEM((n_shot, rows, width), bf16),
            pltpu.VMEM((n_rcv, tiles * rows_e, LANES), bf16),
            pltpu.VMEM((n_rcv, per_tile, tiles + 2 * pad, rows_e, LANES), bf16),
            pltpu.VMEM((n_shot, rows + head, width), bf16),
            pltpu.VMEM((n_shot, rows + head, width), bf16),
            pltpu.VMEM((rows, WIDTH), f32),
            dma((2,)),
            dma((outer_d, chunks)),
            dma((n_shot, chunks)),
            dma((outer_d, chunks)),
            dma((outer_e,)),
            dma((n_rcv,)),
            dma((outer_e,)),
        ],
        compiler_params=pltpu.CompilerParams(collective_id=0, has_side_effects=True),
    )(response, traces)
    return pl.pallas_call(
        arrange,
        out_shape=jax.ShapeDtypeStruct((shots, rcv, samples), bf16),
        in_specs=[vmem],
        out_specs=vmem,
        scratch_shapes=[
            tiled(rows, WIDTH),
            tiled(samples, rcv * shots),
            tiled(shots * rcv, samples),
        ],
    )(y)


def swap_groups(rows, size):
    lane = lax.broadcasted_iota(jnp.int32, rows[0].shape, 1) // size
    step = 1
    while step < len(rows):
        keep = (lane // step) % 2 == 0
        turned = list(rows)
        for i in range(len(rows)):
            if (i // step) % 2 == 0:
                a, b = rows[i], rows[i + step]
                turned[i] = jnp.where(keep, a, pltpu.roll(b, step * size, 1))
                turned[i + step] = jnp.where(keep, pltpu.roll(a, LANES - step * size, 1), b)
        rows = turned
        step *= 2
    return rows


def lag_response(response, lags, y_ref, w_ref):
    shots, rows_e, taps = response.shape
    per_tile = LANES // rows_e
    flat = response.reshape(shots * rows_e, taps)
    row = lax.broadcasted_iota(jnp.int32, (taps, taps), 0)
    col = lax.broadcasted_iota(jnp.int32, (taps, taps), 1)
    put(y_ref, lax.dot_general(
        (row == col).astype(jnp.bfloat16), flat, (((1,), (1,)), ((), ())),
        preferred_element_type=jnp.float32,
    ))
    for tile in range(shots // per_tile):
        rows = [y_ref[tile, pl.ds(j, taps // lags, stride=lags), :] for j in range(lags)]
        for i, value in enumerate(swap_groups(rows, rows_e)):
            w_ref[pl.ds(tile * per_tile + i, taps // lags, stride=shots), :] = value
    return w_ref[...].astype(jnp.bfloat16)


def later(tiles, lag):
    if lag == 0:
        return tiles
    turned = [pltpu.roll(v, lag, 1) for v in tiles]
    lane = lax.broadcasted_iota(jnp.int32, tiles[0].shape, 1)
    before = [jnp.zeros_like(turned[0])] + turned[:-1]
    return [jnp.where(lane >= lag, v, b) for v, b in zip(turned, before)]


def delayed(x, lag):
    if lag == 0:
        return x
    blank = jnp.zeros((x.shape[0], lag), x.dtype)
    return jnp.concatenate([blank, x[:, : x.shape[1] - lag]], axis=1)


def predict_line(
    n_shot, n_rcv, lags, chunks,
    response_hbm, traces_hbm, o_ref,
    response_ref, y_ref, w_ref, gland, tland, a_ref, sh_ref, p_ref, f_ref,
    load, sent, tmate, tpeer, tfar, gline, gside, gover, joined,
):
    shots, rows_e, taps = response_ref.shape
    rows_d, rcv, samples = tland.shape[1:]
    steps = taps // lags
    length = n_rcv // 2
    me_d, me_e = lax.axis_index("shot"), lax.axis_index("rcv")
    in_d, in_e = lax.rem(me_d, 2), lax.rem(me_e, 2)
    out_d, place = me_d // 2, me_e // 2
    mate_d = me_d + 1 - 2 * in_d
    mate_e = me_e + 1 - 2 * in_e
    peer_d = lax.rem(me_d + 2, n_shot)
    far_d = lax.rem(mate_d + 2, n_shot)
    low_bit, high_bit = lax.rem(place, 2), place // 2
    spots = [
        place + (n % 2) * (1 - 2 * low_bit) + (n // 2) * (2 - 4 * high_bit)
        for n in range(length)
    ]
    peers = [
        ((mate_d, me_e), in_d == 1, 0),
        ((peer_d, me_e), out_d == 1, 1),
        ((me_d, mate_e), in_e == 1, 2),
    ]
    peers += [((me_d, 2 * spots[n] + in_e), spots[n] < place, 2 + n) for n in range(1, length)]

    def hold(sem, count):
        @pl.when(count > 0)
        def _():
            pl.semaphore_wait(sem, count)

    barrier = pltpu.get_barrier_semaphore()
    for peer, below, _ in peers:
        @pl.when(jnp.logical_not(below))
        def _():
            pl.semaphore_signal(barrier, inc=1, device_id=peer, device_id_type=MESH)
    fetch_r = pltpu.make_async_copy(response_hbm, response_ref, load.at[0])
    fetch_t = pltpu.make_async_copy(traces_hbm, tland.at[me_d], load.at[1])
    fetch_r.start()
    fetch_t.start()
    with jax.named_scope("barrier"):
        hold(barrier, in_d + out_d + in_e + place)
    for peer, below, kind in peers:
        @pl.when(below)
        def _():
            pl.semaphore_signal(
                joined.at[kind], inc=1, device_id=peer, device_id_type=MESH
            )

    part = rows_d // chunks
    per_half = chunks // 2

    def tpiece(n):
        return pl.ds(lax.rem(n + in_e * per_half, chunks) * part, part)

    def tcopy(owner, n, recv, peer, src=None):
        piece = tpiece(n)
        return pltpu.make_async_remote_copy(
            src_ref=tland.at[owner, piece] if src is None else src.at[piece],
            dst_ref=tland.at[owner, piece],
            send_sem=sent.at[0],
            recv_sem=recv,
            device_id=peer,
            device_id_type=MESH,
        )

    half = steps * shots // 2

    def gcopy(owner, h, recv, peer):
        piece = gland.at[owner, pl.ds(h * half, half)]
        return pltpu.make_async_remote_copy(
            src_ref=piece,
            dst_ref=piece,
            send_sem=sent.at[1],
            recv_sem=recv,
            device_id=peer,
            device_id_type=MESH,
        )

    across = [tcopy(me_d, n, tpeer.at[n], (peer_d, me_e), traces_hbm) for n in range(chunks)]
    beside = pltpu.make_async_remote_copy(
        src_ref=traces_hbm, dst_ref=tland.at[me_d], send_sem=sent.at[0], recv_sem=tmate.at[0],
        device_id=(mate_d, me_e), device_id_type=MESH,
    )
    side = [gcopy(me_e, h, gside.at[h], (me_d, mate_e)) for h in range(2)]
    along = []
    for spot in range(length):
        n = jnp.where(low_bit == spot % 2, 0, 1) + jnp.where(high_bit == spot // 2, 0, 2)
        n = jnp.maximum(n, 1)
        along.append([gcopy(me_e, h, gline.at[n - 1, h], (me_d, 2 * spot + in_e)) for h in range(2)])

    def launch(copies, when):
        @pl.when(when)
        def _():
            for copy in copies:
                copy.start()

    launch(across, out_d == 1)
    launch([beside], in_d == 1)
    with jax.named_scope("fetch_r"):
        fetch_r.wait()
    with jax.named_scope("turn_r"):
        gland[me_e] = lag_response(response_ref[...], lags, y_ref, w_ref)
    launch(side, in_e == 1)
    launch(along[0], place > 0)
    with jax.named_scope("join_m"):
        hold(joined.at[0], 1 - in_d)
    launch([beside], in_d == 0)

    first_z = place == 0
    turn = [
        jnp.where(first_z, 2 + in_d, 1),
        jnp.where(first_z, 3 - in_d, 2),
        jnp.where(first_z, 1, 3),
    ]

    def spot_of(n):
        return sum(jnp.where(n == i, spots[i], 0) for i in range(length))

    def own(n):
        return 2 * spot_of(n) + in_e

    def other(n):
        return 2 * spot_of(n) + 1 - in_e

    def pass_r(n, h):
      with jax.named_scope(f"fr{h}"):
        gcopy(own(n), h, gline.at[n - 1, h], (me_d, mate_e)).wait_recv()
        gcopy(own(n), h, gover.at[n - 1, h], (me_d, mate_e)).start()

    def pass_t(n):
      with jax.named_scope(f"ft{n}"):
        tcopy(peer_d, n, tpeer.at[n], (mate_d, me_e)).wait_recv()
        tcopy(peer_d, n, tfar.at[n], (mate_d, me_e)).start()

    def spread(d, i):
        i = lax.rem(i + in_e, 2)
        with jax.named_scope("spread"):
            e = d * 2 + i
            raw = tland[d, pl.ds(i * rows_e, rows_e)]
            put(a_ref, raw.astype(jnp.float32).reshape(rows_e * rcv, samples))
            for r in range(rcv):
                x = get_rows(a_ref, r, rows_e, rcv).astype(jnp.bfloat16)
                for j in range(lags):
                    sh_ref[e, r, pl.ds(j * rows_e, rows_e), :] = delayed(x, j)

    def far(i):
      with jax.named_scope("wfar"):
        for n in range(i * per_half, (i + 1) * per_half):
            tcopy(far_d, n, tfar.at[n], (mate_d, me_e)).wait_recv()
      spread(far_d, i)

    def meet(n):
      with jax.named_scope("meet"):
        for h in range(2):
            gcopy(other(n), h, gover.at[n - 1, h], (me_d, mate_e)).wait_recv()

    def add(owners, first=False, last=False):
        with jax.named_scope("add"):
            held = jnp.concatenate([gland[e] for e in owners], axis=1)
            for r in range(rcv):
                total = jnp.dot(
                    held,
                    jnp.concatenate([sh_ref[e, r] for e in owners], axis=0),
                    preferred_element_type=jnp.float32,
                )
                if not first:
                    total = p_ref[r] + total
                p_ref[r] = total
                if last:
                    fold(r)

    def fold(r):
        tiles = samples // LANES
        total = [p_ref[r, pl.ds(0, shots), pl.ds(t * LANES, LANES)] for t in range(tiles)]
        for n in range(1, steps):
            lagged = later(
                [p_ref[r, pl.ds(n * shots, shots), pl.ds(t * LANES, LANES)] for t in range(tiles)],
                n * lags,
            )
            total = [v + w for v, w in zip(total, lagged)]
        for t in range(tiles):
            f_ref[t, pl.ds(r, shots, stride=rcv), :] = total[t]

    with jax.named_scope("fetch_t"):
        fetch_t.wait()
    spread(me_d, 0)
    spread(me_d, 1)
    with jax.named_scope("wmate"):
        pltpu.make_async_remote_copy(
            src_ref=traces_hbm, dst_ref=tland.at[mate_d], send_sem=sent.at[0], recv_sem=tmate.at[0],
            device_id=(mate_d, me_e), device_id_type=MESH,
        ).wait_recv()
    spread(mate_d, 0)
    spread(mate_d, 1)
    with jax.named_scope("join_x"):
        hold(joined.at[1], 1 - out_d)
        launch(across, out_d == 0)
    with jax.named_scope("join_y"):
        hold(joined.at[2], 1 - in_e)
        launch(side, in_e == 0)

    def join_z(n):
        with jax.named_scope("join_z"):
            hold(joined.at[2 + n], jnp.where(spots[n] > place, 1, 0))

    for spot in range(1, length):
        launch(along[spot], spot < place)
    for n in range(1, length):
        join_z(n)
        for spot in range(1, length):
            launch(along[spot], jnp.logical_and(spots[n] == spot, spot > place))
    aligned = out_d == high_bit
    pass_t(0)
    pass_r(turn[0], 0)
    pass_r(turn[0], 1)
    pass_t(1)
    pass_r(turn[1], 0)
    pass_r(turn[1], 1)
    spread(peer_d, 0)
    pass_t(2)
    pass_r(turn[2], 0)
    pass_r(turn[2], 1)
    far(0)
    near = [own(0), own(1)]
    rest = [other(0), other(1)]
    add(near, first=True)
    pass_t(3)
    spread(peer_d, 1)
    with jax.named_scope("side"):
        for h in range(2):
            gcopy(other(0), h, gside.at[h], (me_d, mate_e)).wait_recv()

    def choose(yes, no):
        return [jnp.where(first_z, a, b) for a, b in zip(yes, no)]

    def pair(n):
        return [own(n), other(n)]

    aligned = out_d == high_bit
    meet(turn[0])

    @pl.when(aligned)
    def _():
        add(choose(pair(turn[0]), rest))

    far(1)

    @pl.when(jnp.logical_not(aligned))
    def _():
        add(choose(pair(turn[0]), rest))

    meet(turn[1])
    add(choose(pair(turn[1]), pair(2)))
    meet(turn[2])
    add(choose(rest, pair(3)), last=True)
    with jax.named_scope("out"):
        o_ref[...] = get(f_ref).reshape(shots, rcv, samples).astype(jnp.bfloat16)
    with jax.named_scope("wsend"):
        gone = tland.at[pl.ds(0, n_shot - 1)]
        pltpu.make_async_copy(gone, gone, sent.at[0]).wait()
        gone = gland.at[pl.ds(0, n_rcv - 1)]
        pltpu.make_async_copy(gone, gone, sent.at[1]).wait()


def shards(n_shot, n_rcv, response, traces):
    shots, rows_e, taps = response.shape
    rows_d, rcv, samples = traces.shape
    lags = LANES // rows_e
    fits = n_shot == 4 and n_rcv == 8 and rows_d == 2 * rows_e and lags * 8 == taps
    if not fits or shots * (taps // lags) % WIDTH != 0:
        return shards_general(n_shot, n_rcv, response, traces)
    steps = taps // lags
    chunks = 4
    f32, bf16 = jnp.float32, jnp.bfloat16

    def tiled(height, across):
        return pltpu.VMEM((across // LANES, height, LANES), f32)

    dma = pltpu.SemaphoreType.DMA
    vmem = pl.BlockSpec(memory_space=pltpu.VMEM)
    hbm = pl.BlockSpec(memory_space=pl.ANY)
    y = pl.pallas_call(
        functools.partial(predict_line, n_shot, n_rcv, lags, chunks),
        out_shape=pltpu.VMEM((shots, rcv, samples), bf16),
        in_specs=[hbm] * 2,
        out_specs=vmem,
        scratch_shapes=[
            pltpu.VMEM(response.shape, bf16),
            tiled(taps, shots * rows_e),
            pltpu.VMEM((steps * shots, LANES), f32),
            pltpu.VMEM((n_rcv, steps * shots, LANES), bf16),
            pltpu.VMEM((n_shot, rows_d, rcv, samples), bf16),
            tiled(rows_e * rcv, samples),
            pltpu.VMEM((n_rcv, rcv, LANES, samples), bf16),
            pltpu.VMEM((rcv, steps * shots, samples), f32),
            tiled(shots * rcv, samples),
            dma((2,)),
            dma((2,)),
            dma((1,)),
            dma((chunks,)),
            dma((chunks,)),
            dma((n_rcv // 2 - 1, 2)),
            dma((2,)),
            dma((n_rcv // 2 - 1, 2)),
            pltpu.SemaphoreType.REGULAR((n_rcv // 2 + 2,)),
        ],
        compiler_params=pltpu.CompilerParams(collective_id=1, has_side_effects=True),
    )(response, traces)
    return y


def solution(mesh):
    placed = P("shot", "rcv", None)
    return jax.shard_map(
        functools.partial(shards, mesh.shape["shot"], mesh.shape["rcv"]),
        mesh=mesh, in_specs=(placed, placed), out_specs=placed, check_vma=False,
    )
```

```python
import functools

import jax
import jax.numpy as jnp
from jax import lax
from jax.experimental import pallas as pl
from jax.experimental.pallas import tpu as pltpu
from jax.sharding import PartitionSpec as P

MESH = pl.DeviceIdType.MESH
LANES = 128
WIDTH = 256


def put(ref, value):
    for t in range(value.shape[1] // LANES):
        ref[t] = value[:, t * LANES : (t + 1) * LANES]


def put_rows(ref, start, count, stride, value):
    for t in range(value.shape[1] // LANES):
        ref[t, pl.ds(start, count, stride=stride), :] = value[:, t * LANES : (t + 1) * LANES]


def get(ref):
    return jnp.concatenate([ref[t] for t in range(ref.shape[0])], axis=1)


def get_rows(ref, start, count, stride):
    return jnp.concatenate(
        [ref[t, pl.ds(start, count, stride=stride), :] for t in range(ref.shape[0])], axis=1
    )


def turn_response(response, b_ref, y_ref, h_ref):
    shots, rows_e, taps = response.shape
    per_tile = LANES // shots
    tiles = taps // per_tile
    b_ref[:, :taps] = response.astype(jnp.float32).reshape(shots * rows_e, taps)
    stacked = jnp.concatenate(
        [b_ref[pl.ds(k, shots, stride=rows_e), :] for k in range(rows_e)], axis=0
    )
    put(y_ref, stacked.T[:taps])
    by_tap = [get_rows(y_ref, m, tiles, per_tile) for m in range(per_tile)]
    for k in range(rows_e):
        h_ref[pl.ds(k, tiles, stride=rows_e), :] = jnp.concatenate(
            [v[:, k * shots : (k + 1) * shots] for v in by_tap], axis=1
        )
    return h_ref[...].astype(jnp.bfloat16)


def turn_traces(traces, phases, a_ref, z_ref, w_ref):
    rows_d, rcv, samples = traces.shape
    blocks = samples // phases
    put(a_ref, traces.astype(jnp.float32).reshape(rows_d * rcv, samples))
    stacked = jnp.concatenate([get_rows(a_ref, r, rows_d, rcv) for r in range(rcv)], axis=0)
    put(z_ref, stacked.T)
    by_phase = [get_rows(z_ref, v, blocks, phases) for v in range(phases)]
    for r in range(rcv):
        row = jnp.concatenate([z[:, r * rows_d : (r + 1) * rows_d] for z in by_phase], axis=1)
        put_rows(w_ref, r, blocks, rcv, row)
    return get(w_ref).astype(jnp.bfloat16)


def arrange(y_ref, o_ref, acc, z_ref, f_ref):
    shots, rcv, samples = o_ref.shape
    phases = WIDTH // shots
    blocks = samples // phases
    put(acc, y_ref[...].astype(jnp.float32))
    by_rcv = [get_rows(acc, r, blocks, rcv) for r in range(rcv)]
    for u in range(phases):
        row = jnp.concatenate([v[:, u * shots : (u + 1) * shots] for v in by_rcv], axis=1)
        put_rows(z_ref, u, blocks, phases, row)
    turned = get(z_ref).T
    for r in range(rcv):
        put_rows(f_ref, r, shots, rcv, turned[r * shots : (r + 1) * shots])
    o_ref[...] = get(f_ref).reshape(shots, rcv, samples).astype(jnp.bfloat16)


def predict(
    n_shot, n_rcv, chunks,
    response_hbm, traces_hbm, o_ref,
    response_ref, traces_ref, b_ref, y_ref, h_ref, a_ref, z_ref, w_ref,
    x_ref, g_ref, xland, gland, bands, even, odd, acc,
    load, xsend, xrecv, xfwd, gsend, grecv, gfwd,
):
    shots, rows_e, taps = response_ref.shape
    rows_d, rcv, samples = traces_ref.shape
    rows, width = x_ref.shape
    phases = WIDTH // shots
    per_tile = LANES // shots
    tiles = taps // per_tile
    pad = phases // per_tile
    history = taps // phases
    ratio = rows_d // rows_e
    head = history * rcv
    half = rows // 2
    outer_d, outer_e = n_shot // 2, n_rcv // 2
    me_d, me_e = lax.axis_index("shot"), lax.axis_index("rcv")
    in_d, in_e = lax.rem(me_d, 2), lax.rem(me_e, 2)
    out_d, out_e = me_d // 2, me_e // 2
    mate_d = out_d * 2 + 1 - in_d
    mate_e = out_e * 2 + 1 - in_e

    def at_d(step):
        return lax.rem(out_d + step + outer_d, outer_d) * 2 + in_d

    def at_e(step):
        return lax.rem(out_e + step + outer_e, outer_e) * 2 + in_e

    barrier = pltpu.get_barrier_semaphore()
    peers = [(mate_d, me_e), (me_d, mate_e)]
    peers += [(at_d(i), me_e) for i in range(1, outer_d)]
    peers += [(me_d, at_e(i)) for i in range(1, outer_e)]
    for peer in peers:
        pl.semaphore_signal(barrier, inc=1, device_id=peer, device_id_type=MESH)
    fetch_r = pltpu.make_async_copy(response_hbm, response_ref, load.at[0])
    fetch_t = pltpu.make_async_copy(traces_hbm, traces_ref, load.at[1])
    fetch_r.start()
    fetch_t.start()

    part = rows // chunks

    def xcopy(src, owner, c, send, peer):
        piece = pl.ds(c * part, part)
        return pltpu.make_async_remote_copy(
            src_ref=src.at[piece],
            dst_ref=xland.at[owner, piece],
            send_sem=send,
            recv_sem=xrecv.at[owner, c],
            device_id=peer,
            device_id_type=MESH,
        )

    def gcopy(src, owner, send, peer):
        return pltpu.make_async_remote_copy(
            src_ref=src,
            dst_ref=gland.at[owner],
            send_sem=send,
            recv_sem=grecv.at[owner],
            device_id=peer,
            device_id_type=MESH,
        )

    pending = []

    def go(copy):
        copy.start()
        pending.append(copy)

    fetch_r.wait()
    g_ref[...] = turn_response(response_ref[...], b_ref, y_ref, h_ref)
    pl.semaphore_wait(barrier, len(peers))
    order = sorted(range(1, outer_e), key=lambda i: abs(2 * i - outer_e))
    for i in order:
        go(gcopy(g_ref, me_e, gsend.at[i], (me_d, at_e(i))))
    go(gcopy(g_ref, me_e, gsend.at[0], (me_d, mate_e)))
    fetch_t.wait()
    span = samples // chunks
    for c in range(chunks + 1):
        if c < chunks:
            x_ref[pl.ds(c * part, part), :] = turn_traces(
                traces_ref[:, :, pl.ds(c * span, span)], phases, a_ref, z_ref, w_ref
            )
        if c > 0:
            for i in range(1, outer_d):
                go(xcopy(x_ref, me_d, c - 1, xsend.at[i, c - 1], (at_d(i), me_e)))
    for c in range(chunks):
        go(xcopy(x_ref, me_d, c, xsend.at[0, c], (mate_d, me_e)))

    blank = jnp.zeros((rows_e, LANES), jnp.bfloat16)

    def build(e, held):
        padded = [blank] * pad
        padded += [held[a * rows_e : (a + 1) * rows_e] for a in range(tiles)]
        padded += [blank] * (pad + 1)
        for a in range(tiles + 2 * pad):
            for q in range(per_tile):
                value = padded[a]
                if q > 0:
                    value = jnp.concatenate(
                        [padded[a][:, q * shots :], padded[a + 1][:, : q * shots]], axis=1
                    )
                bands[e, q, a] = value

    def place(owner, held, h):
        even[owner, pl.ds(head + h * half, half), :] = held
        odd[owner, pl.ds(head - rcv + h * half, half), :] = held

    def add(owner, h, first=False, last=False):
        left, right = [], []
        for v1 in range(history + 1):
            if v1 % 2 == 0:
                left.append(even[owner, pl.ds(h * half + v1 * rcv, half), :])
            else:
                left.append(odd[owner, pl.ds(h * half + (v1 - 1) * rcv, half), :])
            for v0 in range(phases):
                start = taps - v1 * phases - v0 + phases
                a, q = start // per_tile, start % per_tile
                for k in range(ratio):
                    e = owner * ratio + k
                    right.append(
                        jnp.concatenate([bands[e, q, a + n] for n in range(pad)], axis=1)
                    )
        total = jnp.dot(
            jnp.concatenate(left, axis=1),
            jnp.concatenate(right, axis=0),
            preferred_element_type=jnp.float32,
        )
        mine = pl.ds(h * half, half)
        if not first:
            total = acc[mine, :] + total
        if last:
            o_ref[mine, :] = total.astype(jnp.bfloat16)
        else:
            acc[mine, :] = total

    def forward_x(i, c):
        owner = at_d(-i)
        copy = xcopy(xland.at[owner], owner, c, xfwd.at[i, c], (mate_d, me_e))
        copy.wait_recv()
        go(copy)

    for d in range(n_shot):
        even[d, pl.ds(0, head), :] = jnp.zeros((head, width), jnp.bfloat16)
        odd[d, pl.ds(0, head), :] = jnp.zeros((head, width), jnp.bfloat16)
    for h in range(2):
        place(me_d, x_ref[pl.ds(h * half, half), :], h)
    build(me_e, g_ref[...])

    def arrived(owner):
        for c in range(chunks):
            xcopy(x_ref, owner, c, xsend.at[0, c], (mate_d, me_e)).wait_recv()

    def bring(owner):
        for h in range(2):
            place(owner, xland[owner, pl.ds(h * half, half), :], h)

    todo = [(i, c) for c in range(chunks) for i in range(1, outer_d)]
    for n in range(max(outer_e - 1, len(todo))):
        if n < len(todo):
            forward_x(*todo[n])
        if n < outer_e - 1:
            owner = at_e(-order[n])
            copy = gcopy(gland.at[owner], owner, gfwd.at[n], (me_d, mate_e))
            copy.wait_recv()
            go(copy)
        if n < outer_e - 1:
            build(owner, gland[owner])
    def meet(group):
        owner = group * 2 + 1 - in_e
        gcopy(g_ref, owner, gsend.at[0], (me_d, mate_e)).wait_recv()
        build(owner, gland[owner])

    meet(out_e)
    arrived(mate_d)
    bring(mate_d)
    for i in range(1, outer_d):
        bring(at_d(-i))
    for i in range(1, outer_d):
        owner = lax.rem(out_d - i + outer_d, outer_d) * 2 + 1 - in_d
        arrived(owner)
        bring(owner)

    for n, i in enumerate([0] + order):
        group = lax.rem(out_e - i + outer_e, outer_e)
        if n > 0:
            meet(group)
        if ratio == 2:
            for h in range(2):
                add(group, h, first=n == 0, last=n == outer_e - 1)
    if ratio != 2:
        for d in range(n_shot):
            for h in range(2):
                add(d, h, first=d == 0, last=d == n_shot - 1)
    for copy in pending:
        copy.wait_send()


def shards_general(n_shot, n_rcv, response, traces):
    shots, rows_e, taps = response.shape
    rows_d, rcv, samples = traces.shape
    phases = WIDTH // shots
    blocks = samples // phases
    per_tile = LANES // shots
    tiles = taps // per_tile
    pad = phases // per_tile
    rows = blocks * rcv
    width = phases * rows_d
    chunks = 4
    f32, bf16 = jnp.float32, jnp.bfloat16

    def tiled(height, across):
        return pltpu.VMEM((across // LANES, height, LANES), f32)

    vmem = pl.BlockSpec(memory_space=pltpu.VMEM)
    outer_d, outer_e = n_shot // 2, n_rcv // 2
    head = taps // phases * rcv
    dma = pltpu.SemaphoreType.DMA
    y = pl.pallas_call(
        functools.partial(predict, n_shot, n_rcv, chunks),
        out_shape=jax.ShapeDtypeStruct((rows, WIDTH), bf16),
        in_specs=[pl.BlockSpec(memory_space=pl.ANY)] * 2,
        out_specs=vmem,
        scratch_shapes=[
            pltpu.VMEM(response.shape, bf16),
            pltpu.VMEM(traces.shape, bf16),
            pltpu.VMEM((shots * rows_e, LANES), f32),
            tiled(taps, rows_e * shots),
            pltpu.VMEM((tiles * rows_e, LANES), f32),
            tiled(rows_d * rcv, samples // chunks),
            tiled(samples // chunks, rcv * rows_d),
            tiled(rows // chunks, width),
            pltpu.VMEM((rows, width), bf16),
            pltpu.VMEM((tiles * rows_e, LANES), bf16),
            pltpu.VMEM((n_shot, rows, width), bf16),
            pltpu.VMEM((n_rcv, tiles * rows_e, LANES), bf16),
            pltpu.VMEM((n_rcv, per_tile, tiles + 2 * pad, rows_e, LANES), bf16),
            pltpu.VMEM((n_shot, rows + head, width), bf16),
            pltpu.VMEM((n_shot, rows + head, width), bf16),
            pltpu.VMEM((rows, WIDTH), f32),
            dma((2,)),
            dma((outer_d, chunks)),
            dma((n_shot, chunks)),
            dma((outer_d, chunks)),
            dma((outer_e,)),
            dma((n_rcv,)),
            dma((outer_e,)),
        ],
        compiler_params=pltpu.CompilerParams(collective_id=0, has_side_effects=True),
    )(response, traces)
    return pl.pallas_call(
        arrange,
        out_shape=jax.ShapeDtypeStruct((shots, rcv, samples), bf16),
        in_specs=[vmem],
        out_specs=vmem,
        scratch_shapes=[
            tiled(rows, WIDTH),
            tiled(samples, rcv * shots),
            tiled(shots * rcv, samples),
        ],
    )(y)


def swap_groups(rows, size):
    lane = lax.broadcasted_iota(jnp.int32, rows[0].shape, 1) // size
    step = 1
    while step < len(rows):
        keep = (lane // step) % 2 == 0
        turned = list(rows)
        for i in range(len(rows)):
            if (i // step) % 2 == 0:
                a, b = rows[i], rows[i + step]
                turned[i] = jnp.where(keep, a, pltpu.roll(b, step * size, 1))
                turned[i + step] = jnp.where(keep, pltpu.roll(a, LANES - step * size, 1), b)
        rows = turned
        step *= 2
    return rows


def lag_response(response, lags, y_ref, w_ref):
    shots, rows_e, taps = response.shape
    per_tile = LANES // rows_e
    flat = response.reshape(shots * rows_e, taps)
    row = lax.broadcasted_iota(jnp.int32, (taps, taps), 0)
    col = lax.broadcasted_iota(jnp.int32, (taps, taps), 1)
    put(y_ref, lax.dot_general(
        (row == col).astype(jnp.bfloat16), flat, (((1,), (1,)), ((), ())),
        preferred_element_type=jnp.float32,
    ))
    for tile in range(shots // per_tile):
        rows = [y_ref[tile, pl.ds(j, taps // lags, stride=lags), :] for j in range(lags)]
        for i, value in enumerate(swap_groups(rows, rows_e)):
            w_ref[pl.ds(tile * per_tile + i, taps // lags, stride=shots), :] = value
    return w_ref[...].astype(jnp.bfloat16)


def later(tiles, lag):
    if lag == 0:
        return tiles
    turned = [pltpu.roll(v, lag, 1) for v in tiles]
    lane = lax.broadcasted_iota(jnp.int32, tiles[0].shape, 1)
    before = [jnp.zeros_like(turned[0])] + turned[:-1]
    return [jnp.where(lane >= lag, v, b) for v, b in zip(turned, before)]


def delayed(x, lag):
    if lag == 0:
        return x
    blank = jnp.zeros((x.shape[0], lag), x.dtype)
    return jnp.concatenate([blank, x[:, : x.shape[1] - lag]], axis=1)


def predict_line(
    n_shot, n_rcv, lags, chunks,
    response_hbm, traces_hbm, o_ref,
    response_ref, y_ref, w_ref, gland, tland, a_ref, first_ref, second_ref, p_ref, f_ref,
    load, sent, tmate, tpeer, tfar, gline, gside, gover, joined,
):
    shots, rows_e, taps = response_ref.shape
    rows_d, rcv, samples = tland.shape[1:]
    steps = taps // lags
    length = n_rcv // 2
    me_d, me_e = lax.axis_index("shot"), lax.axis_index("rcv")
    in_d, in_e = lax.rem(me_d, 2), lax.rem(me_e, 2)
    out_d, place = me_d // 2, me_e // 2
    mate_d = me_d + 1 - 2 * in_d
    mate_e = me_e + 1 - 2 * in_e
    peer_d = lax.rem(me_d + 2, n_shot)
    far_d = lax.rem(mate_d + 2, n_shot)
    low_bit, high_bit = lax.rem(place, 2), place // 2
    spots = [
        place + (n % 2) * (1 - 2 * low_bit) + (n // 2) * (2 - 4 * high_bit)
        for n in range(length)
    ]
    peers = [
        ((mate_d, me_e), in_d == 1, 0),
        ((peer_d, me_e), out_d == 1, 1),
        ((me_d, mate_e), in_e == 1, 2),
    ]
    peers += [((me_d, 2 * spots[n] + in_e), spots[n] < place, 2 + n) for n in range(1, length)]

    def hold(sem, count):
        @pl.when(count > 0)
        def _():
            pl.semaphore_wait(sem, count)

    barrier = pltpu.get_barrier_semaphore()
    for peer, below, _ in peers:
        @pl.when(jnp.logical_not(below))
        def _():
            pl.semaphore_signal(barrier, inc=1, device_id=peer, device_id_type=MESH)
    fetch_r = pltpu.make_async_copy(response_hbm, response_ref, load.at[0])
    fetch_t = pltpu.make_async_copy(traces_hbm, tland.at[me_d], load.at[1])
    fetch_r.start()
    fetch_t.start()
    with jax.named_scope("barrier"):
        hold(barrier, in_d + out_d + in_e + place)
    for peer, below, kind in peers:
        @pl.when(below)
        def _():
            pl.semaphore_signal(
                joined.at[kind], inc=1, device_id=peer, device_id_type=MESH
            )

    part = rows_d // chunks
    per_half = chunks // 2

    def tpiece(n):
        return pl.ds(lax.rem(n + in_e * per_half, chunks) * part, part)

    def tcopy(owner, n, recv, peer, src=None):
        piece = tpiece(n)
        return pltpu.make_async_remote_copy(
            src_ref=tland.at[owner, piece] if src is None else src.at[piece],
            dst_ref=tland.at[owner, piece],
            send_sem=sent.at[0],
            recv_sem=recv,
            device_id=peer,
            device_id_type=MESH,
        )

    cuts = 4
    cut = steps * shots // cuts

    def gcopy(owner, h, recv, peer):
        piece = gland.at[owner, pl.ds(h * cut, cut)]
        return pltpu.make_async_remote_copy(
            src_ref=piece,
            dst_ref=piece,
            send_sem=sent.at[1],
            recv_sem=recv,
            device_id=peer,
            device_id_type=MESH,
        )

    def whole(owner, recv):
        return pltpu.make_async_remote_copy(
            src_ref=gland.at[owner],
            dst_ref=gland.at[owner],
            send_sem=sent.at[1],
            recv_sem=recv,
            device_id=(me_d, mate_e),
            device_id_type=MESH,
        )

    across = [tcopy(me_d, n, tpeer.at[n], (peer_d, me_e), traces_hbm) for n in range(chunks)]
    beside = pltpu.make_async_remote_copy(
        src_ref=traces_hbm, dst_ref=tland.at[me_d], send_sem=sent.at[0], recv_sem=tmate.at[0],
        device_id=(mate_d, me_e), device_id_type=MESH,
    )
    side = [gcopy(me_e, h, gside.at[0], (me_d, mate_e)) for h in range(cuts)]
    along = []
    for spot in range(length):
        n = jnp.where(low_bit == spot % 2, 0, 1) + jnp.where(high_bit == spot // 2, 0, 2)
        n = jnp.maximum(n, 1)
        along.append([gcopy(me_e, h, gline.at[n - 1, h], (me_d, 2 * spot + in_e)) for h in range(cuts)])

    def launch(copies, when):
        @pl.when(when)
        def _():
            for copy in copies:
                copy.start()

    launch(across, out_d == 1)
    launch([beside], in_d == 1)
    with jax.named_scope("fetch_r"):
        fetch_r.wait()
    with jax.named_scope("turn_r"):
        gland[me_e] = lag_response(response_ref[...], lags, y_ref, w_ref)
    launch(side, in_e == 1)
    launch(along[0], place > 0)
    with jax.named_scope("join_m"):
        hold(joined.at[0], 1 - in_d)
    launch([beside], in_d == 0)

    first_z = place == 0
    swap = jnp.where(place == 2, 1, 0)
    in_turn = [1 + swap, 2 - swap, 3]
    turn = [
        (jnp.where(first_z, 1 + k % 3, in_turn[k // cuts]), jnp.where(first_z, k // 3, k % cuts))
        for k in range(3 * cuts)
    ]

    def spot_of(n):
        return sum(jnp.where(n == i, spots[i], 0) for i in range(length))

    def own(n):
        return 2 * spot_of(n) + in_e

    def other(n):
        return 2 * spot_of(n) + 1 - in_e

    def pass_r(k):
      with jax.named_scope(f"fr{k}"):
        n, h = turn[k]
        gcopy(own(n), h, gline.at[n - 1, h], (me_d, mate_e)).wait_recv()
        gcopy(own(n), h, gover.at[n - 1], (me_d, mate_e)).start()

    def pass_t(n):
      with jax.named_scope(f"ft{n}"):
        tcopy(peer_d, n, tpeer.at[n], (mate_d, me_e)).wait_recv()
        tcopy(peer_d, n, tfar.at[n], (mate_d, me_e)).start()

    def spreading(d, i):
        raw = tland[d, pl.ds(lax.rem(i + in_e, 2) * rows_e, rows_e)]
        put(a_ref, raw.astype(jnp.float32).reshape(rows_e * rcv, samples))
        out_ref = second_ref if i else first_ref

        def row(r):
            x = get_rows(a_ref, r, rows_e, rcv).astype(jnp.bfloat16)
            for j in range(lags):
                out_ref[d, r, pl.ds(j * rows_e, rows_e), :] = delayed(x, j)

        return row

    def spread(d, i):
        with jax.named_scope("spread"):
            row = spreading(d, i)
            for r in range(rcv):
                row(r)

    def far(i):
        with jax.named_scope("wfar"):
            for n in range(i * per_half, (i + 1) * per_half):
                tcopy(far_d, n, tfar.at[n], (mate_d, me_e)).wait_recv()

    def meet(n):
      with jax.named_scope("meet"):
        whole(2 * spots[n] + 1 - in_e, gover.at[n - 1] if n else gside.at[0]).wait_recv()

    def add(group, second, first=False, last=False, beside=None):
        with jax.named_scope("add"):
            row = None if beside is None else spreading(*beside)
            side = 1 - in_e if second else in_e
            source = second_ref if second else first_ref
            places = [spot_of(n) for n in group]
            held = jnp.concatenate([gland[2 * z + side] for z in places], axis=1)
            for r in range(rcv):
                total = jnp.dot(
                    held,
                    jnp.concatenate([source[z, r] for z in places], axis=0),
                    preferred_element_type=jnp.float32,
                )
                if row is not None:
                    row(r)
                if not first:
                    total = p_ref[r] + total
                p_ref[r] = total
                if last:
                    fold(r)

    def fold(r):
        tiles = samples // LANES
        total = [p_ref[r, pl.ds(0, shots), pl.ds(t * LANES, LANES)] for t in range(tiles)]
        for n in range(1, steps):
            lagged = later(
                [p_ref[r, pl.ds(n * shots, shots), pl.ds(t * LANES, LANES)] for t in range(tiles)],
                n * lags,
            )
            total = [v + w for v, w in zip(total, lagged)]
        for t in range(tiles):
            f_ref[t, pl.ds(r, shots, stride=rcv), :] = total[t]

    with jax.named_scope("fetch_t"):
        fetch_t.wait()
    spread(me_d, 0)
    spread(me_d, 1)
    with jax.named_scope("wmate"):
        pltpu.make_async_remote_copy(
            src_ref=traces_hbm, dst_ref=tland.at[mate_d], send_sem=sent.at[0], recv_sem=tmate.at[0],
            device_id=(mate_d, me_e), device_id_type=MESH,
        ).wait_recv()
    spread(mate_d, 0)
    spread(mate_d, 1)
    for spot in reversed(range(1, length)):
        launch(along[spot], spot < place)
    with jax.named_scope("join_x"):
        hold(joined.at[1], 1 - out_d)
        launch(across, out_d == 0)
    with jax.named_scope("join_y"):
        hold(joined.at[2], 1 - in_e)
        launch(side, in_e == 0)

    def join_z(n):
        with jax.named_scope("join_z"):
            hold(joined.at[2 + n], jnp.where(spots[n] > place, 1, 0))

    for n in range(1, length):
        join_z(n)
        for spot in range(1, length):
            launch(along[spot], jnp.logical_and(spots[n] == spot, spot > place))
    aligned = out_d == high_bit
    aligned = out_d == high_bit

    def half_of(early):
        base = jnp.where(aligned == early, 0, 2)
        return [base, base + 1]

    pass_t(0)
    for k in range(6):
        pass_r(k)
    pass_t(1)
    for k in range(6, 9):
        pass_r(k)
    spread(peer_d, 0)
    pass_t(2)
    for k in range(9, 12):
        pass_r(k)
    far(0)
    add(half_of(True), False, first=True, beside=(far_d, 0))
    pass_t(3)
    add(half_of(False), False, beside=(peer_d, 1))
    far(1)
    spread(far_d, 1)
    meet(0)
    meet(1)
    add([0, 1], True)
    meet(2)
    meet(3)
    add([2, 3], True, last=True)
    with jax.named_scope("out"):
        o_ref[...] = get(f_ref).reshape(shots, rcv, samples).astype(jnp.bfloat16)
    with jax.named_scope("wsend"):
        gone = tland.at[pl.ds(0, n_shot - 1)]
        pltpu.make_async_copy(gone, gone, sent.at[0]).wait()
        gone = gland.at[pl.ds(0, n_rcv - 1)]
        pltpu.make_async_copy(gone, gone, sent.at[1]).wait()


def shards(n_shot, n_rcv, response, traces):
    shots, rows_e, taps = response.shape
    rows_d, rcv, samples = traces.shape
    lags = LANES // rows_e
    fits = n_shot == 4 and n_rcv == 8 and rows_d == 2 * rows_e and lags * 8 == taps
    if not fits or shots * (taps // lags) % WIDTH != 0:
        return shards_general(n_shot, n_rcv, response, traces)
    steps = taps // lags
    chunks = 4
    f32, bf16 = jnp.float32, jnp.bfloat16

    def tiled(height, across):
        return pltpu.VMEM((across // LANES, height, LANES), f32)

    dma = pltpu.SemaphoreType.DMA
    vmem = pl.BlockSpec(memory_space=pltpu.VMEM)
    hbm = pl.BlockSpec(memory_space=pl.ANY)
    y = pl.pallas_call(
        functools.partial(predict_line, n_shot, n_rcv, lags, chunks),
        out_shape=pltpu.VMEM((shots, rcv, samples), bf16),
        in_specs=[hbm] * 2,
        out_specs=vmem,
        scratch_shapes=[
            pltpu.VMEM(response.shape, bf16),
            tiled(taps, shots * rows_e),
            pltpu.VMEM((steps * shots, LANES), f32),
            pltpu.VMEM((n_rcv, steps * shots, LANES), bf16),
            pltpu.VMEM((n_shot, rows_d, rcv, samples), bf16),
            tiled(rows_e * rcv, samples),
            pltpu.VMEM((n_shot, rcv, LANES, samples), bf16),
            pltpu.VMEM((n_shot, rcv, LANES, samples), bf16),
            pltpu.VMEM((rcv, steps * shots, samples), f32),
            tiled(shots * rcv, samples),
            dma((2,)),
            dma((2,)),
            dma((1,)),
            dma((chunks,)),
            dma((chunks,)),
            dma((n_rcv // 2 - 1, 4)),
            dma((1,)),
            dma((n_rcv // 2 - 1,)),
            pltpu.SemaphoreType.REGULAR((n_rcv // 2 + 2,)),
        ],
        compiler_params=pltpu.CompilerParams(collective_id=1, has_side_effects=True),
    )(response, traces)
    return y


def solution(mesh):
    placed = P("shot", "rcv", None)
    return jax.shard_map(
        functools.partial(shards, mesh.shape["shot"], mesh.shape["rcv"]),
        mesh=mesh, in_specs=(placed, placed), out_specs=placed, check_vma=False,
    )
```

```python
import functools

import jax
import jax.numpy as jnp
from jax import lax
from jax.experimental import pallas as pl
from jax.experimental.pallas import tpu as pltpu
from jax.sharding import PartitionSpec as P

MESH = pl.DeviceIdType.MESH
LANES = 128
WIDTH = 256


def put(ref, value):
    for t in range(value.shape[1] // LANES):
        ref[t] = value[:, t * LANES : (t + 1) * LANES]


def put_rows(ref, start, count, stride, value):
    for t in range(value.shape[1] // LANES):
        ref[t, pl.ds(start, count, stride=stride), :] = value[:, t * LANES : (t + 1) * LANES]


def get(ref):
    return jnp.concatenate([ref[t] for t in range(ref.shape[0])], axis=1)


def get_rows(ref, start, count, stride):
    return jnp.concatenate(
        [ref[t, pl.ds(start, count, stride=stride), :] for t in range(ref.shape[0])], axis=1
    )


def turn_response(response, b_ref, y_ref, h_ref):
    shots, rows_e, taps = response.shape
    per_tile = LANES // shots
    tiles = taps // per_tile
    b_ref[:, :taps] = response.astype(jnp.float32).reshape(shots * rows_e, taps)
    stacked = jnp.concatenate(
        [b_ref[pl.ds(k, shots, stride=rows_e), :] for k in range(rows_e)], axis=0
    )
    put(y_ref, stacked.T[:taps])
    by_tap = [get_rows(y_ref, m, tiles, per_tile) for m in range(per_tile)]
    for k in range(rows_e):
        h_ref[pl.ds(k, tiles, stride=rows_e), :] = jnp.concatenate(
            [v[:, k * shots : (k + 1) * shots] for v in by_tap], axis=1
        )
    return h_ref[...].astype(jnp.bfloat16)


def turn_traces(traces, phases, a_ref, z_ref, w_ref):
    rows_d, rcv, samples = traces.shape
    blocks = samples // phases
    put(a_ref, traces.astype(jnp.float32).reshape(rows_d * rcv, samples))
    stacked = jnp.concatenate([get_rows(a_ref, r, rows_d, rcv) for r in range(rcv)], axis=0)
    put(z_ref, stacked.T)
    by_phase = [get_rows(z_ref, v, blocks, phases) for v in range(phases)]
    for r in range(rcv):
        row = jnp.concatenate([z[:, r * rows_d : (r + 1) * rows_d] for z in by_phase], axis=1)
        put_rows(w_ref, r, blocks, rcv, row)
    return get(w_ref).astype(jnp.bfloat16)


def arrange(y_ref, o_ref, acc, z_ref, f_ref):
    shots, rcv, samples = o_ref.shape
    phases = WIDTH // shots
    blocks = samples // phases
    put(acc, y_ref[...].astype(jnp.float32))
    by_rcv = [get_rows(acc, r, blocks, rcv) for r in range(rcv)]
    for u in range(phases):
        row = jnp.concatenate([v[:, u * shots : (u + 1) * shots] for v in by_rcv], axis=1)
        put_rows(z_ref, u, blocks, phases, row)
    turned = get(z_ref).T
    for r in range(rcv):
        put_rows(f_ref, r, shots, rcv, turned[r * shots : (r + 1) * shots])
    o_ref[...] = get(f_ref).reshape(shots, rcv, samples).astype(jnp.bfloat16)


def predict(
    n_shot, n_rcv, chunks,
    response_hbm, traces_hbm, o_ref,
    response_ref, traces_ref, b_ref, y_ref, h_ref, a_ref, z_ref, w_ref,
    x_ref, g_ref, xland, gland, bands, even, odd, acc,
    load, xsend, xrecv, xfwd, gsend, grecv, gfwd,
):
    shots, rows_e, taps = response_ref.shape
    rows_d, rcv, samples = traces_ref.shape
    rows, width = x_ref.shape
    phases = WIDTH // shots
    per_tile = LANES // shots
    tiles = taps // per_tile
    pad = phases // per_tile
    history = taps // phases
    ratio = rows_d // rows_e
    head = history * rcv
    half = rows // 2
    outer_d, outer_e = n_shot // 2, n_rcv // 2
    me_d, me_e = lax.axis_index("shot"), lax.axis_index("rcv")
    in_d, in_e = lax.rem(me_d, 2), lax.rem(me_e, 2)
    out_d, out_e = me_d // 2, me_e // 2
    mate_d = out_d * 2 + 1 - in_d
    mate_e = out_e * 2 + 1 - in_e

    def at_d(step):
        return lax.rem(out_d + step + outer_d, outer_d) * 2 + in_d

    def at_e(step):
        return lax.rem(out_e + step + outer_e, outer_e) * 2 + in_e

    barrier = pltpu.get_barrier_semaphore()
    peers = [(mate_d, me_e), (me_d, mate_e)]
    peers += [(at_d(i), me_e) for i in range(1, outer_d)]
    peers += [(me_d, at_e(i)) for i in range(1, outer_e)]
    for peer in peers:
        pl.semaphore_signal(barrier, inc=1, device_id=peer, device_id_type=MESH)
    fetch_r = pltpu.make_async_copy(response_hbm, response_ref, load.at[0])
    fetch_t = pltpu.make_async_copy(traces_hbm, traces_ref, load.at[1])
    fetch_r.start()
    fetch_t.start()

    part = rows // chunks

    def xcopy(src, owner, c, send, peer):
        piece = pl.ds(c * part, part)
        return pltpu.make_async_remote_copy(
            src_ref=src.at[piece],
            dst_ref=xland.at[owner, piece],
            send_sem=send,
            recv_sem=xrecv.at[owner, c],
            device_id=peer,
            device_id_type=MESH,
        )

    def gcopy(src, owner, send, peer):
        return pltpu.make_async_remote_copy(
            src_ref=src,
            dst_ref=gland.at[owner],
            send_sem=send,
            recv_sem=grecv.at[owner],
            device_id=peer,
            device_id_type=MESH,
        )

    pending = []

    def go(copy):
        copy.start()
        pending.append(copy)

    fetch_r.wait()
    g_ref[...] = turn_response(response_ref[...], b_ref, y_ref, h_ref)
    pl.semaphore_wait(barrier, len(peers))
    order = sorted(range(1, outer_e), key=lambda i: abs(2 * i - outer_e))
    for i in order:
        go(gcopy(g_ref, me_e, gsend.at[i], (me_d, at_e(i))))
    go(gcopy(g_ref, me_e, gsend.at[0], (me_d, mate_e)))
    fetch_t.wait()
    span = samples // chunks
    for c in range(chunks + 1):
        if c < chunks:
            x_ref[pl.ds(c * part, part), :] = turn_traces(
                traces_ref[:, :, pl.ds(c * span, span)], phases, a_ref, z_ref, w_ref
            )
        if c > 0:
            for i in range(1, outer_d):
                go(xcopy(x_ref, me_d, c - 1, xsend.at[i, c - 1], (at_d(i), me_e)))
    for c in range(chunks):
        go(xcopy(x_ref, me_d, c, xsend.at[0, c], (mate_d, me_e)))

    blank = jnp.zeros((rows_e, LANES), jnp.bfloat16)

    def build(e, held):
        padded = [blank] * pad
        padded += [held[a * rows_e : (a + 1) * rows_e] for a in range(tiles)]
        padded += [blank] * (pad + 1)
        for a in range(tiles + 2 * pad):
            for q in range(per_tile):
                value = padded[a]
                if q > 0:
                    value = jnp.concatenate(
                        [padded[a][:, q * shots :], padded[a + 1][:, : q * shots]], axis=1
                    )
                bands[e, q, a] = value

    def place(owner, held, h):
        even[owner, pl.ds(head + h * half, half), :] = held
        odd[owner, pl.ds(head - rcv + h * half, half), :] = held

    def add(owner, h, first=False, last=False):
        left, right = [], []
        for v1 in range(history + 1):
            if v1 % 2 == 0:
                left.append(even[owner, pl.ds(h * half + v1 * rcv, half), :])
            else:
                left.append(odd[owner, pl.ds(h * half + (v1 - 1) * rcv, half), :])
            for v0 in range(phases):
                start = taps - v1 * phases - v0 + phases
                a, q = start // per_tile, start % per_tile
                for k in range(ratio):
                    e = owner * ratio + k
                    right.append(
                        jnp.concatenate([bands[e, q, a + n] for n in range(pad)], axis=1)
                    )
        total = jnp.dot(
            jnp.concatenate(left, axis=1),
            jnp.concatenate(right, axis=0),
            preferred_element_type=jnp.float32,
        )
        mine = pl.ds(h * half, half)
        if not first:
            total = acc[mine, :] + total
        if last:
            o_ref[mine, :] = total.astype(jnp.bfloat16)
        else:
            acc[mine, :] = total

    def forward_x(i, c):
        owner = at_d(-i)
        copy = xcopy(xland.at[owner], owner, c, xfwd.at[i, c], (mate_d, me_e))
        copy.wait_recv()
        go(copy)

    for d in range(n_shot):
        even[d, pl.ds(0, head), :] = jnp.zeros((head, width), jnp.bfloat16)
        odd[d, pl.ds(0, head), :] = jnp.zeros((head, width), jnp.bfloat16)
    for h in range(2):
        place(me_d, x_ref[pl.ds(h * half, half), :], h)
    build(me_e, g_ref[...])

    def arrived(owner):
        for c in range(chunks):
            xcopy(x_ref, owner, c, xsend.at[0, c], (mate_d, me_e)).wait_recv()

    def bring(owner):
        for h in range(2):
            place(owner, xland[owner, pl.ds(h * half, half), :], h)

    todo = [(i, c) for c in range(chunks) for i in range(1, outer_d)]
    for n in range(max(outer_e - 1, len(todo))):
        if n < len(todo):
            forward_x(*todo[n])
        if n < outer_e - 1:
            owner = at_e(-order[n])
            copy = gcopy(gland.at[owner], owner, gfwd.at[n], (me_d, mate_e))
            copy.wait_recv()
            go(copy)
        if n < outer_e - 1:
            build(owner, gland[owner])
    def meet(group):
        owner = group * 2 + 1 - in_e
        gcopy(g_ref, owner, gsend.at[0], (me_d, mate_e)).wait_recv()
        build(owner, gland[owner])

    meet(out_e)
    arrived(mate_d)
    bring(mate_d)
    for i in range(1, outer_d):
        bring(at_d(-i))
    for i in range(1, outer_d):
        owner = lax.rem(out_d - i + outer_d, outer_d) * 2 + 1 - in_d
        arrived(owner)
        bring(owner)

    for n, i in enumerate([0] + order):
        group = lax.rem(out_e - i + outer_e, outer_e)
        if n > 0:
            meet(group)
        if ratio == 2:
            for h in range(2):
                add(group, h, first=n == 0, last=n == outer_e - 1)
    if ratio != 2:
        for d in range(n_shot):
            for h in range(2):
                add(d, h, first=d == 0, last=d == n_shot - 1)
    for copy in pending:
        copy.wait_send()


def shards_general(n_shot, n_rcv, response, traces):
    shots, rows_e, taps = response.shape
    rows_d, rcv, samples = traces.shape
    phases = WIDTH // shots
    blocks = samples // phases
    per_tile = LANES // shots
    tiles = taps // per_tile
    pad = phases // per_tile
    rows = blocks * rcv
    width = phases * rows_d
    chunks = 4
    f32, bf16 = jnp.float32, jnp.bfloat16

    def tiled(height, across):
        return pltpu.VMEM((across // LANES, height, LANES), f32)

    vmem = pl.BlockSpec(memory_space=pltpu.VMEM)
    outer_d, outer_e = n_shot // 2, n_rcv // 2
    head = taps // phases * rcv
    dma = pltpu.SemaphoreType.DMA
    y = pl.pallas_call(
        functools.partial(predict, n_shot, n_rcv, chunks),
        out_shape=jax.ShapeDtypeStruct((rows, WIDTH), bf16),
        in_specs=[pl.BlockSpec(memory_space=pl.ANY)] * 2,
        out_specs=vmem,
        scratch_shapes=[
            pltpu.VMEM(response.shape, bf16),
            pltpu.VMEM(traces.shape, bf16),
            pltpu.VMEM((shots * rows_e, LANES), f32),
            tiled(taps, rows_e * shots),
            pltpu.VMEM((tiles * rows_e, LANES), f32),
            tiled(rows_d * rcv, samples // chunks),
            tiled(samples // chunks, rcv * rows_d),
            tiled(rows // chunks, width),
            pltpu.VMEM((rows, width), bf16),
            pltpu.VMEM((tiles * rows_e, LANES), bf16),
            pltpu.VMEM((n_shot, rows, width), bf16),
            pltpu.VMEM((n_rcv, tiles * rows_e, LANES), bf16),
            pltpu.VMEM((n_rcv, per_tile, tiles + 2 * pad, rows_e, LANES), bf16),
            pltpu.VMEM((n_shot, rows + head, width), bf16),
            pltpu.VMEM((n_shot, rows + head, width), bf16),
            pltpu.VMEM((rows, WIDTH), f32),
            dma((2,)),
            dma((outer_d, chunks)),
            dma((n_shot, chunks)),
            dma((outer_d, chunks)),
            dma((outer_e,)),
            dma((n_rcv,)),
            dma((outer_e,)),
        ],
        compiler_params=pltpu.CompilerParams(collective_id=0, has_side_effects=True),
    )(response, traces)
    return pl.pallas_call(
        arrange,
        out_shape=jax.ShapeDtypeStruct((shots, rcv, samples), bf16),
        in_specs=[vmem],
        out_specs=vmem,
        scratch_shapes=[
            tiled(rows, WIDTH),
            tiled(samples, rcv * shots),
            tiled(shots * rcv, samples),
        ],
    )(y)


def swap_groups(rows, size):
    lane = lax.broadcasted_iota(jnp.int32, rows[0].shape, 1) // size
    step = 1
    while step < len(rows):
        keep = (lane // step) % 2 == 0
        turned = list(rows)
        for i in range(len(rows)):
            if (i // step) % 2 == 0:
                a, b = rows[i], rows[i + step]
                turned[i] = jnp.where(keep, a, pltpu.roll(b, step * size, 1))
                turned[i + step] = jnp.where(keep, pltpu.roll(a, LANES - step * size, 1), b)
        rows = turned
        step *= 2
    return rows


def lag_response(response, lags, y_ref, w_ref):
    shots, rows_e, taps = response.shape
    per_tile = LANES // rows_e
    flat = response.reshape(shots * rows_e, taps)
    row = lax.broadcasted_iota(jnp.int32, (taps, taps), 0)
    col = lax.broadcasted_iota(jnp.int32, (taps, taps), 1)
    put(y_ref, lax.dot_general(
        (row == col).astype(jnp.bfloat16), flat, (((1,), (1,)), ((), ())),
        preferred_element_type=jnp.float32,
    ))
    for tile in range(shots // per_tile):
        rows = [y_ref[tile, pl.ds(j, taps // lags, stride=lags), :] for j in range(lags)]
        for i, value in enumerate(swap_groups(rows, rows_e)):
            w_ref[pl.ds(tile * per_tile + i, taps // lags, stride=shots), :] = value
    return w_ref[...].astype(jnp.bfloat16)


def later(tiles, lag):
    if lag == 0:
        return tiles
    turned = [pltpu.roll(v, lag, 1) for v in tiles]
    lane = lax.broadcasted_iota(jnp.int32, tiles[0].shape, 1)
    before = [jnp.zeros_like(turned[0])] + turned[:-1]
    return [jnp.where(lane >= lag, v, b) for v, b in zip(turned, before)]


def delayed(x, lag):
    if lag == 0:
        return x
    blank = jnp.zeros((x.shape[0], lag), x.dtype)
    return jnp.concatenate([blank, x[:, : x.shape[1] - lag]], axis=1)


def predict_line(
    n_shot, n_rcv, lags, chunks,
    response_hbm, traces_hbm, o_ref,
    response_ref, y_ref, w_ref, gland, tland, a_ref, first_ref, second_ref, p_ref, f_ref,
    load, sent, tmate, tpeer, tfar, gline, gside, gover, joined,
):
    shots, rows_e, taps = response_ref.shape
    rows_d, rcv, samples = tland.shape[1:]
    steps = taps // lags
    length = n_rcv // 2
    me_d, me_e = lax.axis_index("shot"), lax.axis_index("rcv")
    in_d, in_e = lax.rem(me_d, 2), lax.rem(me_e, 2)
    out_d, place = me_d // 2, me_e // 2
    mate_d = me_d + 1 - 2 * in_d
    mate_e = me_e + 1 - 2 * in_e
    peer_d = lax.rem(me_d + 2, n_shot)
    far_d = lax.rem(mate_d + 2, n_shot)
    low_bit, high_bit = lax.rem(place, 2), place // 2
    spots = [
        place + (n % 2) * (1 - 2 * low_bit) + (n // 2) * (2 - 4 * high_bit)
        for n in range(length)
    ]
    peers = [
        ((mate_d, me_e), in_d == 1, 0),
        ((peer_d, me_e), out_d == 1, 1),
        ((me_d, mate_e), in_e == 1, 2),
    ]
    peers += [((me_d, 2 * spots[n] + in_e), spots[n] < place, 2 + n) for n in range(1, length)]

    def hold(sem, count):
        @pl.when(count > 0)
        def _():
            pl.semaphore_wait(sem, count)

    barrier = pltpu.get_barrier_semaphore()
    for peer, below, _ in peers:
        @pl.when(jnp.logical_not(below))
        def _():
            pl.semaphore_signal(barrier, inc=1, device_id=peer, device_id_type=MESH)
    fetch_r = pltpu.make_async_copy(response_hbm, response_ref, load.at[0])
    fetch_t = pltpu.make_async_copy(traces_hbm, tland.at[me_d], load.at[1])
    fetch_r.start()
    fetch_t.start()
    with jax.named_scope("barrier"):
        hold(barrier, in_d + out_d + in_e + place)
    for peer, below, kind in peers:
        @pl.when(below)
        def _():
            pl.semaphore_signal(
                joined.at[kind], inc=1, device_id=peer, device_id_type=MESH
            )

    part = rows_d // chunks
    per_half = chunks // 2

    def tpiece(n):
        return pl.ds(lax.rem(n + in_e * per_half, chunks) * part, part)

    def tcopy(owner, n, recv, peer, src=None):
        piece = tpiece(n)
        return pltpu.make_async_remote_copy(
            src_ref=tland.at[owner, piece] if src is None else src.at[piece],
            dst_ref=tland.at[owner, piece],
            send_sem=sent.at[0],
            recv_sem=recv,
            device_id=peer,
            device_id_type=MESH,
        )

    cuts = 4
    cut = steps * shots // cuts

    def gcopy(owner, h, recv, peer):
        piece = gland.at[owner, pl.ds(h * cut, cut)]
        return pltpu.make_async_remote_copy(
            src_ref=piece,
            dst_ref=piece,
            send_sem=sent.at[1],
            recv_sem=recv,
            device_id=peer,
            device_id_type=MESH,
        )

    def whole(owner, recv):
        return pltpu.make_async_remote_copy(
            src_ref=gland.at[owner],
            dst_ref=gland.at[owner],
            send_sem=sent.at[1],
            recv_sem=recv,
            device_id=(me_d, mate_e),
            device_id_type=MESH,
        )

    across = [tcopy(me_d, n, tpeer.at[n], (peer_d, me_e), traces_hbm) for n in range(chunks)]
    beside = pltpu.make_async_remote_copy(
        src_ref=traces_hbm, dst_ref=tland.at[me_d], send_sem=sent.at[0], recv_sem=tmate.at[0],
        device_id=(mate_d, me_e), device_id_type=MESH,
    )
    side = [gcopy(me_e, h, gside.at[0], (me_d, mate_e)) for h in range(cuts)]
    along = []
    for spot in range(length):
        n = jnp.where(low_bit == spot % 2, 0, 1) + jnp.where(high_bit == spot // 2, 0, 2)
        n = jnp.maximum(n, 1)
        along.append([gcopy(me_e, h, gline.at[n - 1, h], (me_d, 2 * spot + in_e)) for h in range(cuts)])

    def launch(copies, when):
        @pl.when(when)
        def _():
            for copy in copies:
                copy.start()

    launch(across, out_d == 1)
    launch([beside], in_d == 1)
    with jax.named_scope("fetch_r"):
        fetch_r.wait()
    with jax.named_scope("turn_r"):
        gland[me_e] = lag_response(response_ref[...], lags, y_ref, w_ref)
    launch(side, in_e == 1)
    launch(along[0], place > 0)
    with jax.named_scope("join_m"):
        hold(joined.at[0], 1 - in_d)
    launch([beside], in_d == 0)

    first_z = place == 0
    swap = jnp.where(place == 2, 1, 0)
    in_turn = [1 + swap, 2 - swap, 3]
    turn = [
        (jnp.where(first_z, 1 + k % 3, in_turn[k // cuts]), jnp.where(first_z, k // 3, k % cuts))
        for k in range(3 * cuts)
    ]

    def spot_of(n):
        return sum(jnp.where(n == i, spots[i], 0) for i in range(length))

    def own(n):
        return 2 * spot_of(n) + in_e

    def other(n):
        return 2 * spot_of(n) + 1 - in_e

    def pass_r(k):
      with jax.named_scope(f"fr{k}"):
        n, h = turn[k]
        gcopy(own(n), h, gline.at[n - 1, h], (me_d, mate_e)).wait_recv()
        gcopy(own(n), h, gover.at[h // (cuts // 2)], (me_d, mate_e)).start()

    def pass_t(n):
      with jax.named_scope(f"ft{n}"):
        tcopy(peer_d, n, tpeer.at[n], (mate_d, me_e)).wait_recv()
        tcopy(peer_d, n, tfar.at[n], (mate_d, me_e)).start()

    def spreading(d, i):
        raw = tland[d, pl.ds(lax.rem(i + in_e, 2) * rows_e, rows_e)]
        put(a_ref, raw.astype(jnp.float32).reshape(rows_e * rcv, samples))
        out_ref = second_ref if i else first_ref

        def row(r):
            x = get_rows(a_ref, r, rows_e, rcv).astype(jnp.bfloat16)
            for j in range(lags):
                out_ref[d, r, pl.ds(j * rows_e, rows_e), :] = delayed(x, j)

        return row

    def spread(d, i):
        with jax.named_scope("spread"):
            row = spreading(d, i)
            for r in range(rcv):
                row(r)

    def far(i):
        with jax.named_scope("wfar"):
            for n in range(i * per_half, (i + 1) * per_half):
                tcopy(far_d, n, tfar.at[n], (mate_d, me_e)).wait_recv()

    def meet(part):
      with jax.named_scope("meet"):
        if part == 0:
            whole(2 * place + 1 - in_e, gside.at[0]).wait_recv()
        rows = gland.at[pl.ds(0, length - 1), pl.ds(0, steps * shots // 2)]
        pltpu.make_async_copy(rows, rows, gover.at[part]).wait()

    def gather(rows, beside):
        with jax.named_scope("gather"):
            row = spreading(*beside)
            held = jnp.concatenate([gland[2 * z + in_e] for z in spots], axis=1)
            for n, r in enumerate(rows):
                p_ref[r] = jnp.dot(
                    held,
                    jnp.concatenate([first_ref[z, r] for z in spots], axis=0),
                    preferred_element_type=jnp.float32,
                )
                for i in range(n * rcv // len(rows), (n + 1) * rcv // len(rows)):
                    row(i)

    def close(part):
        with jax.named_scope("close"):
            rows = pl.ds(part * steps * shots // 2, steps * shots // 2)
            held = jnp.concatenate([gland[2 * z + 1 - in_e, rows] for z in spots], axis=1)
            for r in range(rcv):
                p_ref[r, rows] = p_ref[r, rows] + jnp.dot(
                    held,
                    jnp.concatenate([second_ref[z, r] for z in spots], axis=0),
                    preferred_element_type=jnp.float32,
                )
                fold(r, part)

    def fold(r, part):
        tiles = samples // LANES
        total = None
        if part > 0:
            total = [f_ref[t, pl.ds(r, shots, stride=rcv), :] for t in range(tiles)]
        for n in range(part * steps // 2, (part + 1) * steps // 2):
            lagged = later(
                [p_ref[r, pl.ds(n * shots, shots), pl.ds(t * LANES, LANES)] for t in range(tiles)],
                n * lags,
            )
            total = lagged if total is None else [v + w for v, w in zip(total, lagged)]
        for t in range(tiles):
            f_ref[t, pl.ds(r, shots, stride=rcv), :] = total[t]

    with jax.named_scope("fetch_t"):
        fetch_t.wait()
    spread(me_d, 0)
    spread(me_d, 1)
    with jax.named_scope("join_x"):
        hold(joined.at[1], 1 - out_d)
        launch(across, out_d == 0)
    with jax.named_scope("join_y"):
        hold(joined.at[2], 1 - in_e)
        launch(side, in_e == 0)
    for spot in range(1, length):
        n = jnp.where(low_bit == spot % 2, 0, 1) + jnp.where(high_bit == spot // 2, 0, 2)
        with jax.named_scope("join_z"):
            hold(joined.at[2 + jnp.maximum(n, 1)], jnp.where(spot > place, 1, 0))
        launch(along[spot], spot > place)
    for spot in reversed(range(1, length)):
        launch(along[spot], spot < place)
    with jax.named_scope("wmate"):
        pltpu.make_async_remote_copy(
            src_ref=traces_hbm, dst_ref=tland.at[mate_d], send_sem=sent.at[0], recv_sem=tmate.at[0],
            device_id=(mate_d, me_e), device_id_type=MESH,
        ).wait_recv()
    spread(mate_d, 0)
    spread(mate_d, 1)
    pass_t(0)
    for k in range(4):
        pass_r(k)
    pass_t(1)
    spread(peer_d, 0)
    for k in range(4, 9):
        pass_r(k)
    pass_t(2)
    for k in range(9, 12):
        pass_r(k)
    pass_t(3)
    far(0)
    spread(far_d, 0)
    gather(range(rcv // 2), (peer_d, 1))
    far(1)
    gather(range(rcv // 2, rcv), (far_d, 1))
    for part in range(2):
        meet(part)
        close(part)
    with jax.named_scope("out"):
        o_ref[...] = get(f_ref).reshape(shots, rcv, samples).astype(jnp.bfloat16)
    with jax.named_scope("wsend"):
        gone = tland.at[pl.ds(0, n_shot - 1)]
        pltpu.make_async_copy(gone, gone, sent.at[0]).wait()
        gone = gland.at[pl.ds(0, n_rcv - 1)]
        pltpu.make_async_copy(gone, gone, sent.at[1]).wait()


def shards(n_shot, n_rcv, response, traces):
    shots, rows_e, taps = response.shape
    rows_d, rcv, samples = traces.shape
    lags = LANES // rows_e
    fits = n_shot == 4 and n_rcv == 8 and rows_d == 2 * rows_e and lags * 8 == taps
    if not fits or shots * (taps // lags) % WIDTH != 0:
        return shards_general(n_shot, n_rcv, response, traces)
    steps = taps // lags
    chunks = 4
    f32, bf16 = jnp.float32, jnp.bfloat16

    def tiled(height, across):
        return pltpu.VMEM((across // LANES, height, LANES), f32)

    dma = pltpu.SemaphoreType.DMA
    vmem = pl.BlockSpec(memory_space=pltpu.VMEM)
    hbm = pl.BlockSpec(memory_space=pl.ANY)
    y = pl.pallas_call(
        functools.partial(predict_line, n_shot, n_rcv, lags, chunks),
        out_shape=pltpu.VMEM((shots, rcv, samples), bf16),
        in_specs=[hbm] * 2,
        out_specs=vmem,
        scratch_shapes=[
            pltpu.VMEM(response.shape, bf16),
            tiled(taps, shots * rows_e),
            pltpu.VMEM((steps * shots, LANES), f32),
            pltpu.VMEM((n_rcv, steps * shots, LANES), bf16),
            pltpu.VMEM((n_shot, rows_d, rcv, samples), bf16),
            tiled(rows_e * rcv, samples),
            pltpu.VMEM((n_shot, rcv, LANES, samples), bf16),
            pltpu.VMEM((n_shot, rcv, LANES, samples), bf16),
            pltpu.VMEM((rcv, steps * shots, samples), f32),
            tiled(shots * rcv, samples),
            dma((2,)),
            dma((2,)),
            dma((1,)),
            dma((chunks,)),
            dma((chunks,)),
            dma((n_rcv // 2 - 1, 4)),
            dma((1,)),
            dma((2,)),
            pltpu.SemaphoreType.REGULAR((n_rcv // 2 + 2,)),
        ],
        compiler_params=pltpu.CompilerParams(collective_id=1, has_side_effects=True),
    )(response, traces)
    return y


def solution(mesh):
    placed = P("shot", "rcv", None)
    return jax.shard_map(
        functools.partial(shards, mesh.shape["shot"], mesh.shape["rcv"]),
        mesh=mesh, in_specs=(placed, placed), out_specs=placed, check_vma=False,
    )
```

```python
import functools

import jax
import jax.numpy as jnp
from jax import lax
from jax.experimental import pallas as pl
from jax.experimental.pallas import tpu as pltpu
from jax.sharding import PartitionSpec as P

MESH = pl.DeviceIdType.MESH
LANES = 128
WIDTH = 256


def put(ref, value):
    for t in range(value.shape[1] // LANES):
        ref[t] = value[:, t * LANES : (t + 1) * LANES]


def put_rows(ref, start, count, stride, value):
    for t in range(value.shape[1] // LANES):
        ref[t, pl.ds(start, count, stride=stride), :] = value[:, t * LANES : (t + 1) * LANES]


def get(ref):
    return jnp.concatenate([ref[t] for t in range(ref.shape[0])], axis=1)


def get_rows(ref, start, count, stride):
    return jnp.concatenate(
        [ref[t, pl.ds(start, count, stride=stride), :] for t in range(ref.shape[0])], axis=1
    )


def turn_response(response, b_ref, y_ref, h_ref):
    shots, rows_e, taps = response.shape
    per_tile = LANES // shots
    tiles = taps // per_tile
    b_ref[:, :taps] = response.astype(jnp.float32).reshape(shots * rows_e, taps)
    stacked = jnp.concatenate(
        [b_ref[pl.ds(k, shots, stride=rows_e), :] for k in range(rows_e)], axis=0
    )
    put(y_ref, stacked.T[:taps])
    by_tap = [get_rows(y_ref, m, tiles, per_tile) for m in range(per_tile)]
    for k in range(rows_e):
        h_ref[pl.ds(k, tiles, stride=rows_e), :] = jnp.concatenate(
            [v[:, k * shots : (k + 1) * shots] for v in by_tap], axis=1
        )
    return h_ref[...].astype(jnp.bfloat16)


def turn_traces(traces, phases, a_ref, z_ref, w_ref):
    rows_d, rcv, samples = traces.shape
    blocks = samples // phases
    put(a_ref, traces.astype(jnp.float32).reshape(rows_d * rcv, samples))
    stacked = jnp.concatenate([get_rows(a_ref, r, rows_d, rcv) for r in range(rcv)], axis=0)
    put(z_ref, stacked.T)
    by_phase = [get_rows(z_ref, v, blocks, phases) for v in range(phases)]
    for r in range(rcv):
        row = jnp.concatenate([z[:, r * rows_d : (r + 1) * rows_d] for z in by_phase], axis=1)
        put_rows(w_ref, r, blocks, rcv, row)
    return get(w_ref).astype(jnp.bfloat16)


def arrange(y_ref, o_ref, acc, z_ref, f_ref):
    shots, rcv, samples = o_ref.shape
    phases = WIDTH // shots
    blocks = samples // phases
    put(acc, y_ref[...].astype(jnp.float32))
    by_rcv = [get_rows(acc, r, blocks, rcv) for r in range(rcv)]
    for u in range(phases):
        row = jnp.concatenate([v[:, u * shots : (u + 1) * shots] for v in by_rcv], axis=1)
        put_rows(z_ref, u, blocks, phases, row)
    turned = get(z_ref).T
    for r in range(rcv):
        put_rows(f_ref, r, shots, rcv, turned[r * shots : (r + 1) * shots])
    o_ref[...] = get(f_ref).reshape(shots, rcv, samples).astype(jnp.bfloat16)


def predict(
    n_shot, n_rcv, chunks,
    response_hbm, traces_hbm, o_ref,
    response_ref, traces_ref, b_ref, y_ref, h_ref, a_ref, z_ref, w_ref,
    x_ref, g_ref, xland, gland, bands, even, odd, acc,
    load, xsend, xrecv, xfwd, gsend, grecv, gfwd,
):
    shots, rows_e, taps = response_ref.shape
    rows_d, rcv, samples = traces_ref.shape
    rows, width = x_ref.shape
    phases = WIDTH // shots
    per_tile = LANES // shots
    tiles = taps // per_tile
    pad = phases // per_tile
    history = taps // phases
    ratio = rows_d // rows_e
    head = history * rcv
    half = rows // 2
    outer_d, outer_e = n_shot // 2, n_rcv // 2
    me_d, me_e = lax.axis_index("shot"), lax.axis_index("rcv")
    in_d, in_e = lax.rem(me_d, 2), lax.rem(me_e, 2)
    out_d, out_e = me_d // 2, me_e // 2
    mate_d = out_d * 2 + 1 - in_d
    mate_e = out_e * 2 + 1 - in_e

    def at_d(step):
        return lax.rem(out_d + step + outer_d, outer_d) * 2 + in_d

    def at_e(step):
        return lax.rem(out_e + step + outer_e, outer_e) * 2 + in_e

    barrier = pltpu.get_barrier_semaphore()
    peers = [(mate_d, me_e), (me_d, mate_e)]
    peers += [(at_d(i), me_e) for i in range(1, outer_d)]
    peers += [(me_d, at_e(i)) for i in range(1, outer_e)]
    for peer in peers:
        pl.semaphore_signal(barrier, inc=1, device_id=peer, device_id_type=MESH)
    fetch_r = pltpu.make_async_copy(response_hbm, response_ref, load.at[0])
    fetch_t = pltpu.make_async_copy(traces_hbm, traces_ref, load.at[1])
    fetch_r.start()
    fetch_t.start()

    part = rows // chunks

    def xcopy(src, owner, c, send, peer):
        piece = pl.ds(c * part, part)
        return pltpu.make_async_remote_copy(
            src_ref=src.at[piece],
            dst_ref=xland.at[owner, piece],
            send_sem=send,
            recv_sem=xrecv.at[owner, c],
            device_id=peer,
            device_id_type=MESH,
        )

    def gcopy(src, owner, send, peer):
        return pltpu.make_async_remote_copy(
            src_ref=src,
            dst_ref=gland.at[owner],
            send_sem=send,
            recv_sem=grecv.at[owner],
            device_id=peer,
            device_id_type=MESH,
        )

    pending = []

    def go(copy):
        copy.start()
        pending.append(copy)

    fetch_r.wait()
    g_ref[...] = turn_response(response_ref[...], b_ref, y_ref, h_ref)
    pl.semaphore_wait(barrier, len(peers))
    order = sorted(range(1, outer_e), key=lambda i: abs(2 * i - outer_e))
    for i in order:
        go(gcopy(g_ref, me_e, gsend.at[i], (me_d, at_e(i))))
    go(gcopy(g_ref, me_e, gsend.at[0], (me_d, mate_e)))
    fetch_t.wait()
    span = samples // chunks
    for c in range(chunks + 1):
        if c < chunks:
            x_ref[pl.ds(c * part, part), :] = turn_traces(
                traces_ref[:, :, pl.ds(c * span, span)], phases, a_ref, z_ref, w_ref
            )
        if c > 0:
            for i in range(1, outer_d):
                go(xcopy(x_ref, me_d, c - 1, xsend.at[i, c - 1], (at_d(i), me_e)))
    for c in range(chunks):
        go(xcopy(x_ref, me_d, c, xsend.at[0, c], (mate_d, me_e)))

    blank = jnp.zeros((rows_e, LANES), jnp.bfloat16)

    def build(e, held):
        padded = [blank] * pad
        padded += [held[a * rows_e : (a + 1) * rows_e] for a in range(tiles)]
        padded += [blank] * (pad + 1)
        for a in range(tiles + 2 * pad):
            for q in range(per_tile):
                value = padded[a]
                if q > 0:
                    value = jnp.concatenate(
                        [padded[a][:, q * shots :], padded[a + 1][:, : q * shots]], axis=1
                    )
                bands[e, q, a] = value

    def place(owner, held, h):
        even[owner, pl.ds(head + h * half, half), :] = held
        odd[owner, pl.ds(head - rcv + h * half, half), :] = held

    def add(owner, h, first=False, last=False):
        left, right = [], []
        for v1 in range(history + 1):
            if v1 % 2 == 0:
                left.append(even[owner, pl.ds(h * half + v1 * rcv, half), :])
            else:
                left.append(odd[owner, pl.ds(h * half + (v1 - 1) * rcv, half), :])
            for v0 in range(phases):
                start = taps - v1 * phases - v0 + phases
                a, q = start // per_tile, start % per_tile
                for k in range(ratio):
                    e = owner * ratio + k
                    right.append(
                        jnp.concatenate([bands[e, q, a + n] for n in range(pad)], axis=1)
                    )
        total = jnp.dot(
            jnp.concatenate(left, axis=1),
            jnp.concatenate(right, axis=0),
            preferred_element_type=jnp.float32,
        )
        mine = pl.ds(h * half, half)
        if not first:
            total = acc[mine, :] + total
        if last:
            o_ref[mine, :] = total.astype(jnp.bfloat16)
        else:
            acc[mine, :] = total

    def forward_x(i, c):
        owner = at_d(-i)
        copy = xcopy(xland.at[owner], owner, c, xfwd.at[i, c], (mate_d, me_e))
        copy.wait_recv()
        go(copy)

    for d in range(n_shot):
        even[d, pl.ds(0, head), :] = jnp.zeros((head, width), jnp.bfloat16)
        odd[d, pl.ds(0, head), :] = jnp.zeros((head, width), jnp.bfloat16)
    for h in range(2):
        place(me_d, x_ref[pl.ds(h * half, half), :], h)
    build(me_e, g_ref[...])

    def arrived(owner):
        for c in range(chunks):
            xcopy(x_ref, owner, c, xsend.at[0, c], (mate_d, me_e)).wait_recv()

    def bring(owner):
        for h in range(2):
            place(owner, xland[owner, pl.ds(h * half, half), :], h)

    todo = [(i, c) for c in range(chunks) for i in range(1, outer_d)]
    for n in range(max(outer_e - 1, len(todo))):
        if n < len(todo):
            forward_x(*todo[n])
        if n < outer_e - 1:
            owner = at_e(-order[n])
            copy = gcopy(gland.at[owner], owner, gfwd.at[n], (me_d, mate_e))
            copy.wait_recv()
            go(copy)
        if n < outer_e - 1:
            build(owner, gland[owner])
    def meet(group):
        owner = group * 2 + 1 - in_e
        gcopy(g_ref, owner, gsend.at[0], (me_d, mate_e)).wait_recv()
        build(owner, gland[owner])

    meet(out_e)
    arrived(mate_d)
    bring(mate_d)
    for i in range(1, outer_d):
        bring(at_d(-i))
    for i in range(1, outer_d):
        owner = lax.rem(out_d - i + outer_d, outer_d) * 2 + 1 - in_d
        arrived(owner)
        bring(owner)

    for n, i in enumerate([0] + order):
        group = lax.rem(out_e - i + outer_e, outer_e)
        if n > 0:
            meet(group)
        if ratio == 2:
            for h in range(2):
                add(group, h, first=n == 0, last=n == outer_e - 1)
    if ratio != 2:
        for d in range(n_shot):
            for h in range(2):
                add(d, h, first=d == 0, last=d == n_shot - 1)
    for copy in pending:
        copy.wait_send()


def shards_general(n_shot, n_rcv, response, traces):
    shots, rows_e, taps = response.shape
    rows_d, rcv, samples = traces.shape
    phases = WIDTH // shots
    blocks = samples // phases
    per_tile = LANES // shots
    tiles = taps // per_tile
    pad = phases // per_tile
    rows = blocks * rcv
    width = phases * rows_d
    chunks = 4
    f32, bf16 = jnp.float32, jnp.bfloat16

    def tiled(height, across):
        return pltpu.VMEM((across // LANES, height, LANES), f32)

    vmem = pl.BlockSpec(memory_space=pltpu.VMEM)
    outer_d, outer_e = n_shot // 2, n_rcv // 2
    head = taps // phases * rcv
    dma = pltpu.SemaphoreType.DMA
    y = pl.pallas_call(
        functools.partial(predict, n_shot, n_rcv, chunks),
        out_shape=jax.ShapeDtypeStruct((rows, WIDTH), bf16),
        in_specs=[pl.BlockSpec(memory_space=pl.ANY)] * 2,
        out_specs=vmem,
        scratch_shapes=[
            pltpu.VMEM(response.shape, bf16),
            pltpu.VMEM(traces.shape, bf16),
            pltpu.VMEM((shots * rows_e, LANES), f32),
            tiled(taps, rows_e * shots),
            pltpu.VMEM((tiles * rows_e, LANES), f32),
            tiled(rows_d * rcv, samples // chunks),
            tiled(samples // chunks, rcv * rows_d),
            tiled(rows // chunks, width),
            pltpu.VMEM((rows, width), bf16),
            pltpu.VMEM((tiles * rows_e, LANES), bf16),
            pltpu.VMEM((n_shot, rows, width), bf16),
            pltpu.VMEM((n_rcv, tiles * rows_e, LANES), bf16),
            pltpu.VMEM((n_rcv, per_tile, tiles + 2 * pad, rows_e, LANES), bf16),
            pltpu.VMEM((n_shot, rows + head, width), bf16),
            pltpu.VMEM((n_shot, rows + head, width), bf16),
            pltpu.VMEM((rows, WIDTH), f32),
            dma((2,)),
            dma((outer_d, chunks)),
            dma((n_shot, chunks)),
            dma((outer_d, chunks)),
            dma((outer_e,)),
            dma((n_rcv,)),
            dma((outer_e,)),
        ],
        compiler_params=pltpu.CompilerParams(collective_id=0, has_side_effects=True),
    )(response, traces)
    return pl.pallas_call(
        arrange,
        out_shape=jax.ShapeDtypeStruct((shots, rcv, samples), bf16),
        in_specs=[vmem],
        out_specs=vmem,
        scratch_shapes=[
            tiled(rows, WIDTH),
            tiled(samples, rcv * shots),
            tiled(shots * rcv, samples),
        ],
    )(y)


def swap_groups(rows, size):
    lane = lax.broadcasted_iota(jnp.int32, rows[0].shape, 1) // size
    step = 1
    while step < len(rows):
        keep = (lane // step) % 2 == 0
        turned = list(rows)
        for i in range(len(rows)):
            if (i // step) % 2 == 0:
                a, b = rows[i], rows[i + step]
                turned[i] = jnp.where(keep, a, pltpu.roll(b, step * size, 1))
                turned[i + step] = jnp.where(keep, pltpu.roll(a, LANES - step * size, 1), b)
        rows = turned
        step *= 2
    return rows


def lag_response(response, lags, b_ref, y_ref, w_ref):
    shots, rows_e, taps = response.shape
    per_tile = LANES // rows_e
    b_ref[:, :taps] = response.reshape(shots * rows_e, taps).astype(jnp.float32)
    for tile in range(shots // per_tile):
        y_ref[tile] = b_ref[pl.ds(tile * LANES, LANES), :].T[:taps]
        rows = [y_ref[tile, pl.ds(j, taps // lags, stride=lags), :] for j in range(lags)]
        for i, value in enumerate(swap_groups(rows, rows_e)):
            w_ref[pl.ds(tile * per_tile + i, taps // lags, stride=shots), :] = value
    return w_ref[...].astype(jnp.bfloat16)


def delayed(x, lag):
    if lag == 0:
        return x
    blank = jnp.zeros((x.shape[0], lag), x.dtype)
    return jnp.concatenate([blank, x[:, : x.shape[1] - lag]], axis=1)


def predict_line(
    n_shot, n_rcv, lags, chunks,
    response_hbm, traces_hbm, o_ref,
    response_ref, b_ref, y_ref, w_ref, gland, tland, a_ref, first_ref, second_ref, p_ref, part_ref, f_ref,
    load, sent, tmate, tpeer, tfar, gline, gside, gover, joined,
):
    shots, rows_e, taps = response_ref.shape
    rows_d, rcv, samples = tland.shape[1:]
    steps = taps // lags
    length = n_rcv // 2
    me_d, me_e = lax.axis_index("shot"), lax.axis_index("rcv")
    in_d, in_e = lax.rem(me_d, 2), lax.rem(me_e, 2)
    out_d, place = me_d // 2, me_e // 2
    mate_d = me_d + 1 - 2 * in_d
    mate_e = me_e + 1 - 2 * in_e
    peer_d = lax.rem(me_d + 2, n_shot)
    far_d = lax.rem(mate_d + 2, n_shot)
    low_bit, high_bit = lax.rem(place, 2), place // 2
    spots = [
        place + (n % 2) * (1 - 2 * low_bit) + (n // 2) * (2 - 4 * high_bit)
        for n in range(length)
    ]
    peers = [
        ((mate_d, me_e), in_d == 1, 0),
        ((peer_d, me_e), out_d == 1, 1),
        ((me_d, mate_e), in_e == 1, 2),
    ]
    peers += [((me_d, 2 * spots[n] + in_e), spots[n] < place, 2 + n) for n in range(1, length)]

    def hold(sem, count):
        @pl.when(count > 0)
        def _():
            pl.semaphore_wait(sem, count)

    barrier = pltpu.get_barrier_semaphore()
    for peer, below, _ in peers:
        @pl.when(jnp.logical_not(below))
        def _():
            pl.semaphore_signal(barrier, inc=1, device_id=peer, device_id_type=MESH)
    fetch_r = pltpu.make_async_copy(response_hbm, response_ref, load.at[0])
    fetch_t = pltpu.make_async_copy(traces_hbm, tland.at[me_d], load.at[1])
    fetch_r.start()
    fetch_t.start()
    with jax.named_scope("barrier"):
        hold(barrier, in_d + out_d + in_e + place)
    for peer, below, kind in peers:
        @pl.when(below)
        def _():
            pl.semaphore_signal(
                joined.at[kind], inc=1, device_id=peer, device_id_type=MESH
            )

    part = rows_d // chunks
    per_half = chunks // 2

    def tpiece(n):
        return pl.ds(lax.rem(n + in_e * per_half, chunks) * part, part)

    def tcopy(owner, n, recv, peer, src=None):
        piece = tpiece(n)
        return pltpu.make_async_remote_copy(
            src_ref=tland.at[owner, piece] if src is None else src.at[piece],
            dst_ref=tland.at[owner, piece],
            send_sem=sent.at[0],
            recv_sem=recv,
            device_id=peer,
            device_id_type=MESH,
        )

    cuts = 4
    cut = steps * shots // cuts

    def gcopy(owner, h, recv, peer):
        piece = gland.at[owner, pl.ds(h * cut, cut)]
        return pltpu.make_async_remote_copy(
            src_ref=piece,
            dst_ref=piece,
            send_sem=sent.at[1],
            recv_sem=recv,
            device_id=peer,
            device_id_type=MESH,
        )

    def whole(owner, recv):
        return pltpu.make_async_remote_copy(
            src_ref=gland.at[owner],
            dst_ref=gland.at[owner],
            send_sem=sent.at[1],
            recv_sem=recv,
            device_id=(me_d, mate_e),
            device_id_type=MESH,
        )

    across = [tcopy(me_d, n, tpeer.at[n], (peer_d, me_e), traces_hbm) for n in range(chunks)]
    beside = pltpu.make_async_remote_copy(
        src_ref=traces_hbm, dst_ref=tland.at[me_d], send_sem=sent.at[0], recv_sem=tmate.at[0],
        device_id=(mate_d, me_e), device_id_type=MESH,
    )
    side = [gcopy(me_e, h, gside.at[0], (me_d, mate_e)) for h in range(cuts)]
    along = []
    for spot in range(length):
        n = jnp.where(low_bit == spot % 2, 0, 1) + jnp.where(high_bit == spot // 2, 0, 2)
        n = jnp.maximum(n, 1)
        along.append([gcopy(me_e, h, gline.at[n - 1, h], (me_d, 2 * spot + in_e)) for h in range(cuts)])

    def launch(copies, when):
        @pl.when(when)
        def _():
            for copy in copies:
                copy.start()

    launch(across, out_d == 1)
    launch([beside], in_d == 1)
    with jax.named_scope("fetch_r"):
        fetch_r.wait()
    with jax.named_scope("turn_r"):
        gland[me_e] = lag_response(response_ref[...], lags, b_ref, y_ref, w_ref)
    launch(side, in_e == 1)
    launch(along[0], place > 0)
    with jax.named_scope("join_m"):
        hold(joined.at[0], 1 - in_d)
    launch([beside], in_d == 0)

    first_z = place == 0
    swap = jnp.where(place == 2, 1, 0)
    flip = jnp.where(jnp.logical_or(place == 3, jnp.logical_and(place == 1, in_d == 1)), 1, 0)
    in_turn = [1 + swap, 2 - swap + flip, 3 - flip]
    mixed = [
        (1, 0), (1, 1), (2, 0), (1, 2), (3, 0), (3, 1), (2, 1), (1, 3), (3, 2), (2, 2), (3, 3), (2, 3)
    ]
    late = jnp.logical_and(place == 1, in_d == 0)
    paired = [(1, h) for h in range(cuts)]
    paired += [(n, h) for part in range(2) for n in (2, 3) for h in (2 * part, 2 * part + 1)]
    turn = [
        (
            jnp.where(first_z, mixed[k][0], jnp.where(late, paired[k][0], in_turn[k // cuts])),
            jnp.where(first_z, mixed[k][1], jnp.where(late, paired[k][1], k % cuts)),
        )
        for k in range(3 * cuts)
    ]

    def spot_of(n):
        return sum(jnp.where(n == i, spots[i], 0) for i in range(length))

    def own(n):
        return 2 * spot_of(n) + in_e

    def other(n):
        return 2 * spot_of(n) + 1 - in_e

    def pass_r(k):
      with jax.named_scope(f"fr{k}"):
        n, h = turn[k]
        gcopy(own(n), h, gline.at[n - 1, h], (me_d, mate_e)).wait_recv()
        gcopy(own(n), h, gover.at[h // (cuts // 2)], (me_d, mate_e)).start()

    def pass_t(n):
      with jax.named_scope(f"ft{n}"):
        tcopy(peer_d, n, tpeer.at[n], (mate_d, me_e)).wait_recv()
        tcopy(peer_d, n, tfar.at[n // per_half], (mate_d, me_e)).start()

    def spreading(d, i):
        raw = tland[d, pl.ds(lax.rem(i + in_e, 2) * rows_e, rows_e)]
        put(a_ref, raw.astype(jnp.float32).reshape(rows_e * rcv, samples))
        out_ref = second_ref if i else first_ref

        def row(r):
            x = get_rows(a_ref, r, rows_e, rcv).astype(jnp.bfloat16)
            for j in range(lags):
                out_ref[d, r, pl.ds(j * rows_e, rows_e), :] = delayed(x, j)

        return row

    def spread(d, i):
        with jax.named_scope("spread"):
            row = spreading(d, i)
            for r in range(rcv):
                row(r)

    def far(i):
        with jax.named_scope("wfar"):
            landed = tland.at[far_d, pl.ds(lax.rem(i + in_e, 2) * rows_e, rows_e)]
            pltpu.make_async_copy(landed, landed, tfar.at[i]).wait()

    def meet(part):
      with jax.named_scope("meet"):
        if part == 0:
            whole(2 * place + 1 - in_e, gside.at[0]).wait_recv()
        rows = gland.at[pl.ds(0, length - 1), pl.ds(0, steps * shots // 2)]
        pltpu.make_async_copy(rows, rows, gover.at[part]).wait()

    def gather(rows, beside):
        with jax.named_scope("gather"):
            row = spreading(*beside)
            held = jnp.concatenate([gland[2 * z + in_e] for z in spots], axis=1)
            for n, r in enumerate(rows):
                p_ref[r] = jnp.dot(
                    held,
                    jnp.concatenate([first_ref[z, r] for z in spots], axis=0),
                    preferred_element_type=jnp.float32,
                )
                for i in range(n * rcv // len(rows), (n + 1) * rcv // len(rows)):
                    row(i)

    def close(part):
        with jax.named_scope("close"):
            count = steps // 2
            rows = pl.ds(part * count * shots, count * shots)
            held = jnp.concatenate([gland[2 * z + 1 - in_e, rows] for z in spots], axis=1)
            lane = lax.broadcasted_iota(jnp.int32, (shots, LANES), 1)
            for r in range(rcv):
                before = [0.0] * count
                for c in range(samples // WIDTH):
                    cols = pl.ds(c * WIDTH, WIDTH)
                    total = p_ref[r, rows, cols] + jnp.dot(
                        held,
                        jnp.concatenate([second_ref[z, r, :, cols] for z in spots], axis=0),
                        preferred_element_type=jnp.float32,
                    )
                    for t in range(WIDTH // LANES):
                        at = c * WIDTH // LANES + t
                        tile = pl.ds(at * LANES, LANES)
                        value = None if part == 0 else part_ref[r, :, tile]
                        for n in range(count):
                            lag = (part * count + n) * lags
                            x = total[n * shots : (n + 1) * shots, t * LANES : (t + 1) * LANES]
                            if lag > 0:
                                turned = pltpu.roll(x, lag, 1)
                                x = jnp.where(lane >= lag, turned, before[n])
                                before[n] = turned
                            value = x if value is None else value + x
                        if part == 0:
                            part_ref[r, :, tile] = value
                        else:
                            f_ref[at, pl.ds(r, shots, stride=rcv), :] = value

    with jax.named_scope("fetch_t"):
        fetch_t.wait()
    spread(me_d, 0)
    spread(me_d, 1)
    with jax.named_scope("join_x"):
        hold(joined.at[1], 1 - out_d)
        launch(across, out_d == 0)
    with jax.named_scope("join_y"):
        hold(joined.at[2], 1 - in_e)
        launch(side, in_e == 0)
    for spot in range(1, length):
        n = jnp.where(low_bit == spot % 2, 0, 1) + jnp.where(high_bit == spot // 2, 0, 2)
        with jax.named_scope("join_z"):
            hold(joined.at[2 + jnp.maximum(n, 1)], jnp.where(spot > place, 1, 0))
        launch(along[spot], spot > place)
    for spot in reversed(range(1, length)):
        launch(along[spot], spot < place)
    with jax.named_scope("wmate"):
        pltpu.make_async_remote_copy(
            src_ref=traces_hbm, dst_ref=tland.at[mate_d], send_sem=sent.at[0], recv_sem=tmate.at[0],
            device_id=(mate_d, me_e), device_id_type=MESH,
        ).wait_recv()
    spread(mate_d, 0)
    spread(mate_d, 1)
    pass_t(0)
    for k in range(4):
        pass_r(k)
    pass_t(1)
    spread(peer_d, 0)
    for k in range(4, 9):
        pass_r(k)
    pass_t(2)
    for k in range(9, 12):
        pass_r(k)
    pass_t(3)
    far(0)
    spread(far_d, 0)
    gather(range(rcv // 2), (peer_d, 1))
    far(1)
    gather(range(rcv // 2, rcv), (far_d, 1))
    for part in range(2):
        meet(part)
        close(part)
    with jax.named_scope("out"):
        o_ref[...] = get(f_ref).reshape(shots, rcv, samples).astype(jnp.bfloat16)
    with jax.named_scope("wsend"):
        gone = tland.at[pl.ds(0, n_shot - 1)]
        pltpu.make_async_copy(gone, gone, sent.at[0]).wait()
        gone = gland.at[pl.ds(0, n_rcv - 1)]
        pltpu.make_async_copy(gone, gone, sent.at[1]).wait()


def shards(n_shot, n_rcv, response, traces):
    shots, rows_e, taps = response.shape
    rows_d, rcv, samples = traces.shape
    lags = LANES // rows_e
    fits = n_shot == 4 and n_rcv == 8 and rows_d == 2 * rows_e and lags * 8 == taps
    if not fits or shots * (taps // lags) % WIDTH != 0:
        return shards_general(n_shot, n_rcv, response, traces)
    steps = taps // lags
    chunks = 4
    f32, bf16 = jnp.float32, jnp.bfloat16

    def tiled(height, across):
        return pltpu.VMEM((across // LANES, height, LANES), f32)

    dma = pltpu.SemaphoreType.DMA
    vmem = pl.BlockSpec(memory_space=pltpu.VMEM)
    hbm = pl.BlockSpec(memory_space=pl.ANY)
    y = pl.pallas_call(
        functools.partial(predict_line, n_shot, n_rcv, lags, chunks),
        out_shape=pltpu.VMEM((shots, rcv, samples), bf16),
        in_specs=[hbm] * 2,
        out_specs=vmem,
        scratch_shapes=[
            pltpu.VMEM(response.shape, bf16),
            pltpu.VMEM((shots * rows_e, LANES), f32),
            tiled(taps, shots * rows_e),
            pltpu.VMEM((steps * shots, LANES), f32),
            pltpu.VMEM((n_rcv, steps * shots, LANES), bf16),
            pltpu.VMEM((n_shot, rows_d, rcv, samples), bf16),
            tiled(rows_e * rcv, samples),
            pltpu.VMEM((n_shot, rcv, LANES, samples), bf16),
            pltpu.VMEM((n_shot, rcv, LANES, samples), bf16),
            pltpu.VMEM((rcv, steps * shots, samples), f32),
            pltpu.VMEM((rcv, shots, samples), f32),
            tiled(shots * rcv, samples),
            dma((2,)),
            dma((2,)),
            dma((1,)),
            dma((chunks,)),
            dma((2,)),
            dma((n_rcv // 2 - 1, 4)),
            dma((1,)),
            dma((2,)),
            pltpu.SemaphoreType.REGULAR((n_rcv // 2 + 2,)),
        ],
        compiler_params=pltpu.CompilerParams(collective_id=1, has_side_effects=True),
    )(response, traces)
    return y


def solution(mesh):
    placed = P("shot", "rcv", None)
    return jax.shard_map(
        functools.partial(shards, mesh.shape["shot"], mesh.shape["rcv"]),
        mesh=mesh, in_specs=(placed, placed), out_specs=placed, check_vma=False,
    )
```

```python
import functools

import jax
import jax.numpy as jnp
from jax import lax
from jax.experimental import pallas as pl
from jax.experimental.pallas import tpu as pltpu
from jax.sharding import PartitionSpec as P

MESH = pl.DeviceIdType.MESH
LANES = 128
WIDTH = 256


def put(ref, value):
    for t in range(value.shape[1] // LANES):
        ref[t] = value[:, t * LANES : (t + 1) * LANES]


def put_rows(ref, start, count, stride, value):
    for t in range(value.shape[1] // LANES):
        ref[t, pl.ds(start, count, stride=stride), :] = value[:, t * LANES : (t + 1) * LANES]


def get(ref):
    return jnp.concatenate([ref[t] for t in range(ref.shape[0])], axis=1)


def get_rows(ref, start, count, stride):
    return jnp.concatenate(
        [ref[t, pl.ds(start, count, stride=stride), :] for t in range(ref.shape[0])], axis=1
    )


def turn_response(response, b_ref, y_ref, h_ref):
    shots, rows_e, taps = response.shape
    per_tile = LANES // shots
    tiles = taps // per_tile
    b_ref[:, :taps] = response.astype(jnp.float32).reshape(shots * rows_e, taps)
    stacked = jnp.concatenate(
        [b_ref[pl.ds(k, shots, stride=rows_e), :] for k in range(rows_e)], axis=0
    )
    put(y_ref, stacked.T[:taps])
    by_tap = [get_rows(y_ref, m, tiles, per_tile) for m in range(per_tile)]
    for k in range(rows_e):
        h_ref[pl.ds(k, tiles, stride=rows_e), :] = jnp.concatenate(
            [v[:, k * shots : (k + 1) * shots] for v in by_tap], axis=1
        )
    return h_ref[...].astype(jnp.bfloat16)


def turn_traces(traces, phases, a_ref, z_ref, w_ref):
    rows_d, rcv, samples = traces.shape
    blocks = samples // phases
    put(a_ref, traces.astype(jnp.float32).reshape(rows_d * rcv, samples))
    stacked = jnp.concatenate([get_rows(a_ref, r, rows_d, rcv) for r in range(rcv)], axis=0)
    put(z_ref, stacked.T)
    by_phase = [get_rows(z_ref, v, blocks, phases) for v in range(phases)]
    for r in range(rcv):
        row = jnp.concatenate([z[:, r * rows_d : (r + 1) * rows_d] for z in by_phase], axis=1)
        put_rows(w_ref, r, blocks, rcv, row)
    return get(w_ref).astype(jnp.bfloat16)


def arrange(y_ref, o_ref, acc, z_ref, f_ref):
    shots, rcv, samples = o_ref.shape
    phases = WIDTH // shots
    blocks = samples // phases
    put(acc, y_ref[...].astype(jnp.float32))
    by_rcv = [get_rows(acc, r, blocks, rcv) for r in range(rcv)]
    for u in range(phases):
        row = jnp.concatenate([v[:, u * shots : (u + 1) * shots] for v in by_rcv], axis=1)
        put_rows(z_ref, u, blocks, phases, row)
    turned = get(z_ref).T
    for r in range(rcv):
        put_rows(f_ref, r, shots, rcv, turned[r * shots : (r + 1) * shots])
    o_ref[...] = get(f_ref).reshape(shots, rcv, samples).astype(jnp.bfloat16)


def predict(
    n_shot, n_rcv, chunks,
    response_hbm, traces_hbm, o_ref,
    response_ref, traces_ref, b_ref, y_ref, h_ref, a_ref, z_ref, w_ref,
    x_ref, g_ref, xland, gland, bands, even, odd, acc,
    load, xsend, xrecv, xfwd, gsend, grecv, gfwd,
):
    shots, rows_e, taps = response_ref.shape
    rows_d, rcv, samples = traces_ref.shape
    rows, width = x_ref.shape
    phases = WIDTH // shots
    per_tile = LANES // shots
    tiles = taps // per_tile
    pad = phases // per_tile
    history = taps // phases
    ratio = rows_d // rows_e
    head = history * rcv
    half = rows // 2
    outer_d, outer_e = n_shot // 2, n_rcv // 2
    me_d, me_e = lax.axis_index("shot"), lax.axis_index("rcv")
    in_d, in_e = lax.rem(me_d, 2), lax.rem(me_e, 2)
    out_d, out_e = me_d // 2, me_e // 2
    mate_d = out_d * 2 + 1 - in_d
    mate_e = out_e * 2 + 1 - in_e

    def at_d(step):
        return lax.rem(out_d + step + outer_d, outer_d) * 2 + in_d

    def at_e(step):
        return lax.rem(out_e + step + outer_e, outer_e) * 2 + in_e

    barrier = pltpu.get_barrier_semaphore()
    peers = [(mate_d, me_e), (me_d, mate_e)]
    peers += [(at_d(i), me_e) for i in range(1, outer_d)]
    peers += [(me_d, at_e(i)) for i in range(1, outer_e)]
    for peer in peers:
        pl.semaphore_signal(barrier, inc=1, device_id=peer, device_id_type=MESH)
    fetch_r = pltpu.make_async_copy(response_hbm, response_ref, load.at[0])
    fetch_t = pltpu.make_async_copy(traces_hbm, traces_ref, load.at[1])
    fetch_r.start()
    fetch_t.start()

    part = rows // chunks

    def xcopy(src, owner, c, send, peer):
        piece = pl.ds(c * part, part)
        return pltpu.make_async_remote_copy(
            src_ref=src.at[piece],
            dst_ref=xland.at[owner, piece],
            send_sem=send,
            recv_sem=xrecv.at[owner, c],
            device_id=peer,
            device_id_type=MESH,
        )

    def gcopy(src, owner, send, peer):
        return pltpu.make_async_remote_copy(
            src_ref=src,
            dst_ref=gland.at[owner],
            send_sem=send,
            recv_sem=grecv.at[owner],
            device_id=peer,
            device_id_type=MESH,
        )

    pending = []

    def go(copy):
        copy.start()
        pending.append(copy)

    fetch_r.wait()
    g_ref[...] = turn_response(response_ref[...], b_ref, y_ref, h_ref)
    pl.semaphore_wait(barrier, len(peers))
    order = sorted(range(1, outer_e), key=lambda i: abs(2 * i - outer_e))
    for i in order:
        go(gcopy(g_ref, me_e, gsend.at[i], (me_d, at_e(i))))
    go(gcopy(g_ref, me_e, gsend.at[0], (me_d, mate_e)))
    fetch_t.wait()
    span = samples // chunks
    for c in range(chunks + 1):
        if c < chunks:
            x_ref[pl.ds(c * part, part), :] = turn_traces(
                traces_ref[:, :, pl.ds(c * span, span)], phases, a_ref, z_ref, w_ref
            )
        if c > 0:
            for i in range(1, outer_d):
                go(xcopy(x_ref, me_d, c - 1, xsend.at[i, c - 1], (at_d(i), me_e)))
    for c in range(chunks):
        go(xcopy(x_ref, me_d, c, xsend.at[0, c], (mate_d, me_e)))

    blank = jnp.zeros((rows_e, LANES), jnp.bfloat16)

    def build(e, held):
        padded = [blank] * pad
        padded += [held[a * rows_e : (a + 1) * rows_e] for a in range(tiles)]
        padded += [blank] * (pad + 1)
        for a in range(tiles + 2 * pad):
            for q in range(per_tile):
                value = padded[a]
                if q > 0:
                    value = jnp.concatenate(
                        [padded[a][:, q * shots :], padded[a + 1][:, : q * shots]], axis=1
                    )
                bands[e, q, a] = value

    def place(owner, held, h):
        even[owner, pl.ds(head + h * half, half), :] = held
        odd[owner, pl.ds(head - rcv + h * half, half), :] = held

    def add(owner, h, first=False, last=False):
        left, right = [], []
        for v1 in range(history + 1):
            if v1 % 2 == 0:
                left.append(even[owner, pl.ds(h * half + v1 * rcv, half), :])
            else:
                left.append(odd[owner, pl.ds(h * half + (v1 - 1) * rcv, half), :])
            for v0 in range(phases):
                start = taps - v1 * phases - v0 + phases
                a, q = start // per_tile, start % per_tile
                for k in range(ratio):
                    e = owner * ratio + k
                    right.append(
                        jnp.concatenate([bands[e, q, a + n] for n in range(pad)], axis=1)
                    )
        total = jnp.dot(
            jnp.concatenate(left, axis=1),
            jnp.concatenate(right, axis=0),
            preferred_element_type=jnp.float32,
        )
        mine = pl.ds(h * half, half)
        if not first:
            total = acc[mine, :] + total
        if last:
            o_ref[mine, :] = total.astype(jnp.bfloat16)
        else:
            acc[mine, :] = total

    def forward_x(i, c):
        owner = at_d(-i)
        copy = xcopy(xland.at[owner], owner, c, xfwd.at[i, c], (mate_d, me_e))
        copy.wait_recv()
        go(copy)

    for d in range(n_shot):
        even[d, pl.ds(0, head), :] = jnp.zeros((head, width), jnp.bfloat16)
        odd[d, pl.ds(0, head), :] = jnp.zeros((head, width), jnp.bfloat16)
    for h in range(2):
        place(me_d, x_ref[pl.ds(h * half, half), :], h)
    build(me_e, g_ref[...])

    def arrived(owner):
        for c in range(chunks):
            xcopy(x_ref, owner, c, xsend.at[0, c], (mate_d, me_e)).wait_recv()

    def bring(owner):
        for h in range(2):
            place(owner, xland[owner, pl.ds(h * half, half), :], h)

    todo = [(i, c) for c in range(chunks) for i in range(1, outer_d)]
    for n in range(max(outer_e - 1, len(todo))):
        if n < len(todo):
            forward_x(*todo[n])
        if n < outer_e - 1:
            owner = at_e(-order[n])
            copy = gcopy(gland.at[owner], owner, gfwd.at[n], (me_d, mate_e))
            copy.wait_recv()
            go(copy)
        if n < outer_e - 1:
            build(owner, gland[owner])
    def meet(group):
        owner = group * 2 + 1 - in_e
        gcopy(g_ref, owner, gsend.at[0], (me_d, mate_e)).wait_recv()
        build(owner, gland[owner])

    meet(out_e)
    arrived(mate_d)
    bring(mate_d)
    for i in range(1, outer_d):
        bring(at_d(-i))
    for i in range(1, outer_d):
        owner = lax.rem(out_d - i + outer_d, outer_d) * 2 + 1 - in_d
        arrived(owner)
        bring(owner)

    for n, i in enumerate([0] + order):
        group = lax.rem(out_e - i + outer_e, outer_e)
        if n > 0:
            meet(group)
        if ratio == 2:
            for h in range(2):
                add(group, h, first=n == 0, last=n == outer_e - 1)
    if ratio != 2:
        for d in range(n_shot):
            for h in range(2):
                add(d, h, first=d == 0, last=d == n_shot - 1)
    for copy in pending:
        copy.wait_send()


def shards_general(n_shot, n_rcv, response, traces):
    shots, rows_e, taps = response.shape
    rows_d, rcv, samples = traces.shape
    phases = WIDTH // shots
    blocks = samples // phases
    per_tile = LANES // shots
    tiles = taps // per_tile
    pad = phases // per_tile
    rows = blocks * rcv
    width = phases * rows_d
    chunks = 4
    f32, bf16 = jnp.float32, jnp.bfloat16

    def tiled(height, across):
        return pltpu.VMEM((across // LANES, height, LANES), f32)

    vmem = pl.BlockSpec(memory_space=pltpu.VMEM)
    outer_d, outer_e = n_shot // 2, n_rcv // 2
    head = taps // phases * rcv
    dma = pltpu.SemaphoreType.DMA
    y = pl.pallas_call(
        functools.partial(predict, n_shot, n_rcv, chunks),
        out_shape=jax.ShapeDtypeStruct((rows, WIDTH), bf16),
        in_specs=[pl.BlockSpec(memory_space=pl.ANY)] * 2,
        out_specs=vmem,
        scratch_shapes=[
            pltpu.VMEM(response.shape, bf16),
            pltpu.VMEM(traces.shape, bf16),
            pltpu.VMEM((shots * rows_e, LANES), f32),
            tiled(taps, rows_e * shots),
            pltpu.VMEM((tiles * rows_e, LANES), f32),
            tiled(rows_d * rcv, samples // chunks),
            tiled(samples // chunks, rcv * rows_d),
            tiled(rows // chunks, width),
            pltpu.VMEM((rows, width), bf16),
            pltpu.VMEM((tiles * rows_e, LANES), bf16),
            pltpu.VMEM((n_shot, rows, width), bf16),
            pltpu.VMEM((n_rcv, tiles * rows_e, LANES), bf16),
            pltpu.VMEM((n_rcv, per_tile, tiles + 2 * pad, rows_e, LANES), bf16),
            pltpu.VMEM((n_shot, rows + head, width), bf16),
            pltpu.VMEM((n_shot, rows + head, width), bf16),
            pltpu.VMEM((rows, WIDTH), f32),
            dma((2,)),
            dma((outer_d, chunks)),
            dma((n_shot, chunks)),
            dma((outer_d, chunks)),
            dma((outer_e,)),
            dma((n_rcv,)),
            dma((outer_e,)),
        ],
        compiler_params=pltpu.CompilerParams(collective_id=0, has_side_effects=True),
    )(response, traces)
    return pl.pallas_call(
        arrange,
        out_shape=jax.ShapeDtypeStruct((shots, rcv, samples), bf16),
        in_specs=[vmem],
        out_specs=vmem,
        scratch_shapes=[
            tiled(rows, WIDTH),
            tiled(samples, rcv * shots),
            tiled(shots * rcv, samples),
        ],
    )(y)


def swap_groups(rows, size):
    lane = lax.broadcasted_iota(jnp.int32, rows[0].shape, 1) // size
    step = 1
    while step < len(rows):
        keep = (lane // step) % 2 == 0
        turned = list(rows)
        for i in range(len(rows)):
            if (i // step) % 2 == 0:
                a, b = rows[i], rows[i + step]
                turned[i] = jnp.where(keep, a, pltpu.roll(b, step * size, 1))
                turned[i + step] = jnp.where(keep, pltpu.roll(a, LANES - step * size, 1), b)
        rows = turned
        step *= 2
    return rows


def lag_response(response, lags, b_ref, y_ref, w_ref):
    shots, rows_e, taps = response.shape
    per_tile = LANES // rows_e
    b_ref[:, :taps] = response.reshape(shots * rows_e, taps).astype(jnp.float32)
    for tile in range(shots // per_tile):
        turned = b_ref[pl.ds(tile * LANES, LANES), :].T
        y_ref[tile] = jnp.concatenate([turned[lags:taps], turned[:lags]])
        rows = [y_ref[tile, pl.ds(j, taps // lags, stride=lags), :] for j in range(lags)]
        for i, value in enumerate(swap_groups(rows, rows_e)):
            w_ref[pl.ds(tile * per_tile + i, taps // lags, stride=shots), :] = value
    return w_ref[...].astype(jnp.bfloat16)


def delayed(x, lag):
    if lag == 0:
        return x
    blank = jnp.zeros((x.shape[0], lag), x.dtype)
    return jnp.concatenate([blank, x[:, : x.shape[1] - lag]], axis=1)


def predict_line(
    n_shot, n_rcv, lags, chunks,
    response_hbm, traces_hbm, o_ref,
    response_ref, b_ref, y_ref, w_ref, gland, tland, a_ref, first_ref, second_ref, p_ref, part_ref, f_ref,
    load, sent, tmate, tpeer, tfar, gline, gside, gover, joined,
):
    shots, rows_e, taps = response_ref.shape
    rows_d, rcv, samples = tland.shape[1:]
    steps = taps // lags
    length = n_rcv // 2
    me_d, me_e = lax.axis_index("shot"), lax.axis_index("rcv")
    in_d, in_e = lax.rem(me_d, 2), lax.rem(me_e, 2)
    out_d, place = me_d // 2, me_e // 2
    mate_d = me_d + 1 - 2 * in_d
    mate_e = me_e + 1 - 2 * in_e
    peer_d = lax.rem(me_d + 2, n_shot)
    far_d = lax.rem(mate_d + 2, n_shot)
    low_bit, high_bit = lax.rem(place, 2), place // 2
    spots = [
        place + (n % 2) * (1 - 2 * low_bit) + (n // 2) * (2 - 4 * high_bit)
        for n in range(length)
    ]
    peers = [
        ((mate_d, me_e), in_d == 1, 0),
        ((peer_d, me_e), out_d == 1, 1),
        ((me_d, mate_e), in_e == 1, 2),
    ]
    peers += [((me_d, 2 * spots[n] + in_e), spots[n] < place, 2 + n) for n in range(1, length)]

    def hold(sem, count):
        @pl.when(count > 0)
        def _():
            pl.semaphore_wait(sem, count)

    barrier = pltpu.get_barrier_semaphore()
    for peer, below, _ in peers:
        @pl.when(jnp.logical_not(below))
        def _():
            pl.semaphore_signal(barrier, inc=1, device_id=peer, device_id_type=MESH)
    fetch_r = pltpu.make_async_copy(response_hbm, response_ref, load.at[0])
    fetch_t = pltpu.make_async_copy(traces_hbm, tland.at[me_d], load.at[1])
    share = shots // 4
    for i in range(4):
        some = pl.ds(i * share, share)
        pltpu.make_async_copy(response_hbm.at[some], response_ref.at[some], load.at[0]).start()
    fetch_t.start()
    with jax.named_scope("barrier"):
        hold(barrier, in_d + out_d + in_e + place)
    for peer, below, kind in peers:
        @pl.when(below)
        def _():
            pl.semaphore_signal(
                joined.at[kind], inc=1, device_id=peer, device_id_type=MESH
            )

    part = rows_d // chunks
    per_half = chunks // 2

    def tpiece(n):
        return pl.ds(lax.rem(n + in_e * per_half, chunks) * part, part)

    def tcopy(owner, n, recv, peer, src=None):
        piece = tpiece(n)
        return pltpu.make_async_remote_copy(
            src_ref=tland.at[owner, piece] if src is None else src.at[piece],
            dst_ref=tland.at[owner, piece],
            send_sem=sent.at[0],
            recv_sem=recv,
            device_id=peer,
            device_id_type=MESH,
        )

    cuts = 4
    cut = steps * shots // cuts

    def gcopy(owner, h, recv, peer):
        piece = gland.at[owner, pl.ds(h * cut, cut)]
        return pltpu.make_async_remote_copy(
            src_ref=piece,
            dst_ref=piece,
            send_sem=sent.at[1],
            recv_sem=recv,
            device_id=peer,
            device_id_type=MESH,
        )

    def whole(owner, recv):
        return pltpu.make_async_remote_copy(
            src_ref=gland.at[owner],
            dst_ref=gland.at[owner],
            send_sem=sent.at[1],
            recv_sem=recv,
            device_id=(me_d, mate_e),
            device_id_type=MESH,
        )

    across = [tcopy(me_d, n, tpeer.at[n], (peer_d, me_e), traces_hbm) for n in range(chunks)]
    beside = pltpu.make_async_remote_copy(
        src_ref=traces_hbm, dst_ref=tland.at[me_d], send_sem=sent.at[0], recv_sem=tmate.at[0],
        device_id=(mate_d, me_e), device_id_type=MESH,
    )
    side = [gcopy(me_e, h, gside.at[0], (me_d, mate_e)) for h in range(cuts)]
    along = []
    for spot in range(length):
        n = jnp.where(low_bit == spot % 2, 0, 1) + jnp.where(high_bit == spot // 2, 0, 2)
        n = jnp.maximum(n, 1)
        along.append([gcopy(me_e, h, gline.at[n - 1, h], (me_d, 2 * spot + in_e)) for h in range(cuts)])

    def launch(copies, when):
        @pl.when(when)
        def _():
            for copy in copies:
                copy.start()

    launch(across, out_d == 1)
    launch([beside], in_d == 1)
    with jax.named_scope("fetch_r"):
        fetch_r.wait()
    with jax.named_scope("turn_r"):
        gland[me_e] = lag_response(response_ref[...], lags, b_ref, y_ref, w_ref)
    launch(side, in_e == 1)
    launch(along[0], place > 0)
    with jax.named_scope("join_m"):
        hold(joined.at[0], 1 - in_d)
    launch([beside], in_d == 0)

    first_z = place == 0
    swap = jnp.where(place == 2, 1, 0)
    flip = jnp.where(jnp.logical_or(place == 3, jnp.logical_and(place == 1, in_d == 1)), 1, 0)
    in_turn = [1 + swap, 2 - swap + flip, 3 - flip]
    mixed = [
        (1, 0), (1, 1), (2, 0), (1, 2), (3, 0), (3, 1), (2, 1), (1, 3), (3, 2), (2, 2), (3, 3), (2, 3)
    ]
    late = jnp.logical_and(place == 1, in_d == 0)
    paired = [(1, h) for h in range(cuts)]
    paired += [(n, h) for part in range(2) for n in (2, 3) for h in (2 * part, 2 * part + 1)]
    turn = [
        (
            jnp.where(first_z, mixed[k][0], jnp.where(late, paired[k][0], in_turn[k // cuts])),
            jnp.where(first_z, mixed[k][1], jnp.where(late, paired[k][1], k % cuts)),
        )
        for k in range(3 * cuts)
    ]

    def spot_of(n):
        return sum(jnp.where(n == i, spots[i], 0) for i in range(length))

    def own(n):
        return 2 * spot_of(n) + in_e

    def other(n):
        return 2 * spot_of(n) + 1 - in_e

    def pass_r(k):
      with jax.named_scope(f"fr{k}"):
        n, h = turn[k]
        gcopy(own(n), h, gline.at[n - 1, h], (me_d, mate_e)).wait_recv()
        gcopy(own(n), h, gover.at[h // (cuts // 2)], (me_d, mate_e)).start()

    def pass_t(n):
      with jax.named_scope(f"ft{n}"):
        tcopy(peer_d, n, tpeer.at[n], (mate_d, me_e)).wait_recv()
        tcopy(peer_d, n, tfar.at[n // per_half], (mate_d, me_e)).start()

    def spreading(d, i):
        raw = tland[d, pl.ds(lax.rem(i + in_e, 2) * rows_e, rows_e)]
        put(a_ref, raw.astype(jnp.float32).reshape(rows_e * rcv, samples))
        out_ref = second_ref if i else first_ref

        def row(r):
            x = get_rows(a_ref, r, rows_e, rcv).astype(jnp.bfloat16)
            for j in range(lags):
                out_ref[d, r, pl.ds(j * rows_e, rows_e), :] = delayed(x, j)

        return row

    def spread(d, i):
        with jax.named_scope("spread"):
            row = spreading(d, i)
            for r in range(rcv):
                row(r)

    def far(i):
        with jax.named_scope("wfar"):
            landed = tland.at[far_d, pl.ds(lax.rem(i + in_e, 2) * rows_e, rows_e)]
            pltpu.make_async_copy(landed, landed, tfar.at[i]).wait()

    def meet(part):
      with jax.named_scope("meet"):
        if part == 0:
            whole(2 * place + 1 - in_e, gside.at[0]).wait_recv()
        rows = gland.at[pl.ds(0, length - 1), pl.ds(0, steps * shots // 2)]
        pltpu.make_async_copy(rows, rows, gover.at[part]).wait()

    def gather(rows, beside):
        with jax.named_scope("gather"):
            row = spreading(*beside)
            held = jnp.concatenate([gland[2 * z + in_e] for z in spots], axis=1)
            for n, r in enumerate(rows):
                p_ref[r] = jnp.dot(
                    held,
                    jnp.concatenate([first_ref[z, r] for z in spots], axis=0),
                    preferred_element_type=jnp.float32,
                )
                for i in range(n * rcv // len(rows), (n + 1) * rcv // len(rows)):
                    row(i)

    def close(part):
        with jax.named_scope("close"):
            count = steps // 2
            rows = pl.ds(part * count * shots, count * shots)
            held = jnp.concatenate([gland[2 * z + 1 - in_e, rows] for z in spots], axis=1)
            lane = lax.broadcasted_iota(jnp.int32, (shots, LANES), 1)
            for r in range(rcv):
                before = [0.0] * count
                for c in range(samples // WIDTH):
                    cols = pl.ds(c * WIDTH, WIDTH)
                    total = p_ref[r, rows, cols] + jnp.dot(
                        held,
                        jnp.concatenate([second_ref[z, r, :, cols] for z in spots], axis=0),
                        preferred_element_type=jnp.float32,
                    )
                    for t in range(WIDTH // LANES):
                        at = c * WIDTH // LANES + t
                        tile = pl.ds(at * LANES, LANES)
                        value = None if part == 0 else part_ref[r, :, tile]
                        for n in range(count):
                            lag = (part * count + n + 1) % steps * lags
                            x = total[n * shots : (n + 1) * shots, t * LANES : (t + 1) * LANES]
                            if lag > 0:
                                turned = pltpu.roll(x, lag, 1)
                                x = jnp.where(lane >= lag, turned, before[n])
                                before[n] = turned
                            value = x if value is None else value + x
                        if part == 0:
                            part_ref[r, :, tile] = value
                        else:
                            f_ref[at, pl.ds(r, shots, stride=rcv), :] = value

    with jax.named_scope("fetch_t"):
        fetch_t.wait()
    spread(me_d, 0)
    spread(me_d, 1)
    with jax.named_scope("join_x"):
        hold(joined.at[1], 1 - out_d)
        launch(across, out_d == 0)
    with jax.named_scope("join_y"):
        hold(joined.at[2], 1 - in_e)
        launch(side, in_e == 0)
    for spot in range(1, length):
        n = jnp.where(low_bit == spot % 2, 0, 1) + jnp.where(high_bit == spot // 2, 0, 2)
        with jax.named_scope("join_z"):
            hold(joined.at[2 + jnp.maximum(n, 1)], jnp.where(spot > place, 1, 0))
        launch(along[spot], spot > place)
    for spot in reversed(range(1, length)):
        launch(along[spot], spot < place)
    @pl.when(place == 0)
    def _():
        pass_r(0)

    with jax.named_scope("wmate"):
        pltpu.make_async_remote_copy(
            src_ref=traces_hbm, dst_ref=tland.at[mate_d], send_sem=sent.at[0], recv_sem=tmate.at[0],
            device_id=(mate_d, me_e), device_id_type=MESH,
        ).wait_recv()
    spread(mate_d, 0)
    spread(mate_d, 1)
    pass_t(0)
    @pl.when(place > 0)
    def _():
        pass_r(0)

    for k in range(1, 4):
        pass_r(k)
    pass_t(1)
    spread(peer_d, 0)
    for k in range(4, 9):
        pass_r(k)
    pass_t(2)
    for k in range(9, 12):
        pass_r(k)
    pass_t(3)
    far(0)
    spread(far_d, 0)
    gather(range(rcv // 2), (peer_d, 1))
    far(1)
    gather(range(rcv // 2, rcv), (far_d, 1))
    for part in range(2):
        meet(part)
        close(part)
    with jax.named_scope("out"):
        o_ref[...] = get(f_ref).reshape(shots, rcv, samples).astype(jnp.bfloat16)
    with jax.named_scope("wsend"):
        gone = tland.at[pl.ds(0, n_shot - 1)]
        pltpu.make_async_copy(gone, gone, sent.at[0]).wait()
        gone = gland.at[pl.ds(0, n_rcv - 1)]
        pltpu.make_async_copy(gone, gone, sent.at[1]).wait()


def shards(n_shot, n_rcv, response, traces):
    shots, rows_e, taps = response.shape
    rows_d, rcv, samples = traces.shape
    lags = LANES // rows_e
    fits = n_shot == 4 and n_rcv == 8 and rows_d == 2 * rows_e and lags * 8 == taps
    if not fits or shots * (taps // lags) % WIDTH != 0:
        return shards_general(n_shot, n_rcv, response, traces)
    steps = taps // lags
    chunks = 4
    f32, bf16 = jnp.float32, jnp.bfloat16

    def tiled(height, across):
        return pltpu.VMEM((across // LANES, height, LANES), f32)

    dma = pltpu.SemaphoreType.DMA
    vmem = pl.BlockSpec(memory_space=pltpu.VMEM)
    hbm = pl.BlockSpec(memory_space=pl.ANY)
    y = pl.pallas_call(
        functools.partial(predict_line, n_shot, n_rcv, lags, chunks),
        out_shape=pltpu.VMEM((shots, rcv, samples), bf16),
        in_specs=[hbm] * 2,
        out_specs=vmem,
        scratch_shapes=[
            pltpu.VMEM(response.shape, bf16),
            pltpu.VMEM((shots * rows_e, LANES), f32),
            tiled(taps, shots * rows_e),
            pltpu.VMEM((steps * shots, LANES), f32),
            pltpu.VMEM((n_rcv, steps * shots, LANES), bf16),
            pltpu.VMEM((n_shot, rows_d, rcv, samples), bf16),
            tiled(rows_e * rcv, samples),
            pltpu.VMEM((n_shot, rcv, LANES, samples), bf16),
            pltpu.VMEM((n_shot, rcv, LANES, samples), bf16),
            pltpu.VMEM((rcv, steps * shots, samples), f32),
            pltpu.VMEM((rcv, shots, samples), f32),
            tiled(shots * rcv, samples),
            dma((2,)),
            dma((2,)),
            dma((1,)),
            dma((chunks,)),
            dma((2,)),
            dma((n_rcv // 2 - 1, 4)),
            dma((1,)),
            dma((2,)),
            pltpu.SemaphoreType.REGULAR((n_rcv // 2 + 2,)),
        ],
        compiler_params=pltpu.CompilerParams(collective_id=1, has_side_effects=True),
    )(response, traces)
    return y


def solution(mesh):
    placed = P("shot", "rcv", None)
    return jax.shard_map(
        functools.partial(shards, mesh.shape["shot"], mesh.shape["rcv"]),
        mesh=mesh, in_specs=(placed, placed), out_specs=placed, check_vma=False,
    )
```

```python
import functools

import jax
import jax.numpy as jnp
from jax import lax
from jax.experimental import pallas as pl
from jax.experimental.pallas import tpu as pltpu
from jax.sharding import PartitionSpec as P

MESH = pl.DeviceIdType.MESH
LANES = 128
WIDTH = 256


def put(ref, value):
    for t in range(value.shape[1] // LANES):
        ref[t] = value[:, t * LANES : (t + 1) * LANES]


def put_rows(ref, start, count, stride, value):
    for t in range(value.shape[1] // LANES):
        ref[t, pl.ds(start, count, stride=stride), :] = value[:, t * LANES : (t + 1) * LANES]


def get(ref):
    return jnp.concatenate([ref[t] for t in range(ref.shape[0])], axis=1)


def get_rows(ref, start, count, stride):
    return jnp.concatenate(
        [ref[t, pl.ds(start, count, stride=stride), :] for t in range(ref.shape[0])], axis=1
    )


def turn_response(response, b_ref, y_ref, h_ref):
    shots, rows_e, taps = response.shape
    per_tile = LANES // shots
    tiles = taps // per_tile
    b_ref[:, :taps] = response.astype(jnp.float32).reshape(shots * rows_e, taps)
    stacked = jnp.concatenate(
        [b_ref[pl.ds(k, shots, stride=rows_e), :] for k in range(rows_e)], axis=0
    )
    put(y_ref, stacked.T[:taps])
    by_tap = [get_rows(y_ref, m, tiles, per_tile) for m in range(per_tile)]
    for k in range(rows_e):
        h_ref[pl.ds(k, tiles, stride=rows_e), :] = jnp.concatenate(
            [v[:, k * shots : (k + 1) * shots] for v in by_tap], axis=1
        )
    return h_ref[...].astype(jnp.bfloat16)


def turn_traces(traces, phases, a_ref, z_ref, w_ref):
    rows_d, rcv, samples = traces.shape
    blocks = samples // phases
    put(a_ref, traces.astype(jnp.float32).reshape(rows_d * rcv, samples))
    stacked = jnp.concatenate([get_rows(a_ref, r, rows_d, rcv) for r in range(rcv)], axis=0)
    put(z_ref, stacked.T)
    by_phase = [get_rows(z_ref, v, blocks, phases) for v in range(phases)]
    for r in range(rcv):
        row = jnp.concatenate([z[:, r * rows_d : (r + 1) * rows_d] for z in by_phase], axis=1)
        put_rows(w_ref, r, blocks, rcv, row)
    return get(w_ref).astype(jnp.bfloat16)


def arrange(y_ref, o_ref, acc, z_ref, f_ref):
    shots, rcv, samples = o_ref.shape
    phases = WIDTH // shots
    blocks = samples // phases
    put(acc, y_ref[...].astype(jnp.float32))
    by_rcv = [get_rows(acc, r, blocks, rcv) for r in range(rcv)]
    for u in range(phases):
        row = jnp.concatenate([v[:, u * shots : (u + 1) * shots] for v in by_rcv], axis=1)
        put_rows(z_ref, u, blocks, phases, row)
    turned = get(z_ref).T
    for r in range(rcv):
        put_rows(f_ref, r, shots, rcv, turned[r * shots : (r + 1) * shots])
    o_ref[...] = get(f_ref).reshape(shots, rcv, samples).astype(jnp.bfloat16)


def predict(
    n_shot, n_rcv, chunks,
    response_hbm, traces_hbm, o_ref,
    response_ref, traces_ref, b_ref, y_ref, h_ref, a_ref, z_ref, w_ref,
    x_ref, g_ref, xland, gland, bands, even, odd, acc,
    load, xsend, xrecv, xfwd, gsend, grecv, gfwd,
):
    shots, rows_e, taps = response_ref.shape
    rows_d, rcv, samples = traces_ref.shape
    rows, width = x_ref.shape
    phases = WIDTH // shots
    per_tile = LANES // shots
    tiles = taps // per_tile
    pad = phases // per_tile
    history = taps // phases
    ratio = rows_d // rows_e
    head = history * rcv
    half = rows // 2
    outer_d, outer_e = n_shot // 2, n_rcv // 2
    me_d, me_e = lax.axis_index("shot"), lax.axis_index("rcv")
    in_d, in_e = lax.rem(me_d, 2), lax.rem(me_e, 2)
    out_d, out_e = me_d // 2, me_e // 2
    mate_d = out_d * 2 + 1 - in_d
    mate_e = out_e * 2 + 1 - in_e

    def at_d(step):
        return lax.rem(out_d + step + outer_d, outer_d) * 2 + in_d

    def at_e(step):
        return lax.rem(out_e + step + outer_e, outer_e) * 2 + in_e

    barrier = pltpu.get_barrier_semaphore()
    peers = [(mate_d, me_e), (me_d, mate_e)]
    peers += [(at_d(i), me_e) for i in range(1, outer_d)]
    peers += [(me_d, at_e(i)) for i in range(1, outer_e)]
    for peer in peers:
        pl.semaphore_signal(barrier, inc=1, device_id=peer, device_id_type=MESH)
    fetch_r = pltpu.make_async_copy(response_hbm, response_ref, load.at[0])
    fetch_t = pltpu.make_async_copy(traces_hbm, traces_ref, load.at[1])
    fetch_r.start()
    fetch_t.start()

    part = rows // chunks

    def xcopy(src, owner, c, send, peer):
        piece = pl.ds(c * part, part)
        return pltpu.make_async_remote_copy(
            src_ref=src.at[piece],
            dst_ref=xland.at[owner, piece],
            send_sem=send,
            recv_sem=xrecv.at[owner, c],
            device_id=peer,
            device_id_type=MESH,
        )

    def gcopy(src, owner, send, peer):
        return pltpu.make_async_remote_copy(
            src_ref=src,
            dst_ref=gland.at[owner],
            send_sem=send,
            recv_sem=grecv.at[owner],
            device_id=peer,
            device_id_type=MESH,
        )

    pending = []

    def go(copy):
        copy.start()
        pending.append(copy)

    fetch_r.wait()
    g_ref[...] = turn_response(response_ref[...], b_ref, y_ref, h_ref)
    pl.semaphore_wait(barrier, len(peers))
    order = sorted(range(1, outer_e), key=lambda i: abs(2 * i - outer_e))
    for i in order:
        go(gcopy(g_ref, me_e, gsend.at[i], (me_d, at_e(i))))
    go(gcopy(g_ref, me_e, gsend.at[0], (me_d, mate_e)))
    fetch_t.wait()
    span = samples // chunks
    for c in range(chunks + 1):
        if c < chunks:
            x_ref[pl.ds(c * part, part), :] = turn_traces(
                traces_ref[:, :, pl.ds(c * span, span)], phases, a_ref, z_ref, w_ref
            )
        if c > 0:
            for i in range(1, outer_d):
                go(xcopy(x_ref, me_d, c - 1, xsend.at[i, c - 1], (at_d(i), me_e)))
    for c in range(chunks):
        go(xcopy(x_ref, me_d, c, xsend.at[0, c], (mate_d, me_e)))

    blank = jnp.zeros((rows_e, LANES), jnp.bfloat16)

    def build(e, held):
        padded = [blank] * pad
        padded += [held[a * rows_e : (a + 1) * rows_e] for a in range(tiles)]
        padded += [blank] * (pad + 1)
        for a in range(tiles + 2 * pad):
            for q in range(per_tile):
                value = padded[a]
                if q > 0:
                    value = jnp.concatenate(
                        [padded[a][:, q * shots :], padded[a + 1][:, : q * shots]], axis=1
                    )
                bands[e, q, a] = value

    def place(owner, held, h):
        even[owner, pl.ds(head + h * half, half), :] = held
        odd[owner, pl.ds(head - rcv + h * half, half), :] = held

    def add(owner, h, first=False, last=False):
        left, right = [], []
        for v1 in range(history + 1):
            if v1 % 2 == 0:
                left.append(even[owner, pl.ds(h * half + v1 * rcv, half), :])
            else:
                left.append(odd[owner, pl.ds(h * half + (v1 - 1) * rcv, half), :])
            for v0 in range(phases):
                start = taps - v1 * phases - v0 + phases
                a, q = start // per_tile, start % per_tile
                for k in range(ratio):
                    e = owner * ratio + k
                    right.append(
                        jnp.concatenate([bands[e, q, a + n] for n in range(pad)], axis=1)
                    )
        total = jnp.dot(
            jnp.concatenate(left, axis=1),
            jnp.concatenate(right, axis=0),
            preferred_element_type=jnp.float32,
        )
        mine = pl.ds(h * half, half)
        if not first:
            total = acc[mine, :] + total
        if last:
            o_ref[mine, :] = total.astype(jnp.bfloat16)
        else:
            acc[mine, :] = total

    def forward_x(i, c):
        owner = at_d(-i)
        copy = xcopy(xland.at[owner], owner, c, xfwd.at[i, c], (mate_d, me_e))
        copy.wait_recv()
        go(copy)

    for d in range(n_shot):
        even[d, pl.ds(0, head), :] = jnp.zeros((head, width), jnp.bfloat16)
        odd[d, pl.ds(0, head), :] = jnp.zeros((head, width), jnp.bfloat16)
    for h in range(2):
        place(me_d, x_ref[pl.ds(h * half, half), :], h)
    build(me_e, g_ref[...])

    def arrived(owner):
        for c in range(chunks):
            xcopy(x_ref, owner, c, xsend.at[0, c], (mate_d, me_e)).wait_recv()

    def bring(owner):
        for h in range(2):
            place(owner, xland[owner, pl.ds(h * half, half), :], h)

    todo = [(i, c) for c in range(chunks) for i in range(1, outer_d)]
    for n in range(max(outer_e - 1, len(todo))):
        if n < len(todo):
            forward_x(*todo[n])
        if n < outer_e - 1:
            owner = at_e(-order[n])
            copy = gcopy(gland.at[owner], owner, gfwd.at[n], (me_d, mate_e))
            copy.wait_recv()
            go(copy)
        if n < outer_e - 1:
            build(owner, gland[owner])
    def meet(group):
        owner = group * 2 + 1 - in_e
        gcopy(g_ref, owner, gsend.at[0], (me_d, mate_e)).wait_recv()
        build(owner, gland[owner])

    meet(out_e)
    arrived(mate_d)
    bring(mate_d)
    for i in range(1, outer_d):
        bring(at_d(-i))
    for i in range(1, outer_d):
        owner = lax.rem(out_d - i + outer_d, outer_d) * 2 + 1 - in_d
        arrived(owner)
        bring(owner)

    for n, i in enumerate([0] + order):
        group = lax.rem(out_e - i + outer_e, outer_e)
        if n > 0:
            meet(group)
        if ratio == 2:
            for h in range(2):
                add(group, h, first=n == 0, last=n == outer_e - 1)
    if ratio != 2:
        for d in range(n_shot):
            for h in range(2):
                add(d, h, first=d == 0, last=d == n_shot - 1)
    for copy in pending:
        copy.wait_send()


def shards_general(n_shot, n_rcv, response, traces):
    shots, rows_e, taps = response.shape
    rows_d, rcv, samples = traces.shape
    phases = WIDTH // shots
    blocks = samples // phases
    per_tile = LANES // shots
    tiles = taps // per_tile
    pad = phases // per_tile
    rows = blocks * rcv
    width = phases * rows_d
    chunks = 4
    f32, bf16 = jnp.float32, jnp.bfloat16

    def tiled(height, across):
        return pltpu.VMEM((across // LANES, height, LANES), f32)

    vmem = pl.BlockSpec(memory_space=pltpu.VMEM)
    outer_d, outer_e = n_shot // 2, n_rcv // 2
    head = taps // phases * rcv
    dma = pltpu.SemaphoreType.DMA
    y = pl.pallas_call(
        functools.partial(predict, n_shot, n_rcv, chunks),
        out_shape=jax.ShapeDtypeStruct((rows, WIDTH), bf16),
        in_specs=[pl.BlockSpec(memory_space=pl.ANY)] * 2,
        out_specs=vmem,
        scratch_shapes=[
            pltpu.VMEM(response.shape, bf16),
            pltpu.VMEM(traces.shape, bf16),
            pltpu.VMEM((shots * rows_e, LANES), f32),
            tiled(taps, rows_e * shots),
            pltpu.VMEM((tiles * rows_e, LANES), f32),
            tiled(rows_d * rcv, samples // chunks),
            tiled(samples // chunks, rcv * rows_d),
            tiled(rows // chunks, width),
            pltpu.VMEM((rows, width), bf16),
            pltpu.VMEM((tiles * rows_e, LANES), bf16),
            pltpu.VMEM((n_shot, rows, width), bf16),
            pltpu.VMEM((n_rcv, tiles * rows_e, LANES), bf16),
            pltpu.VMEM((n_rcv, per_tile, tiles + 2 * pad, rows_e, LANES), bf16),
            pltpu.VMEM((n_shot, rows + head, width), bf16),
            pltpu.VMEM((n_shot, rows + head, width), bf16),
            pltpu.VMEM((rows, WIDTH), f32),
            dma((2,)),
            dma((outer_d, chunks)),
            dma((n_shot, chunks)),
            dma((outer_d, chunks)),
            dma((outer_e,)),
            dma((n_rcv,)),
            dma((outer_e,)),
        ],
        compiler_params=pltpu.CompilerParams(collective_id=0, has_side_effects=True),
    )(response, traces)
    return pl.pallas_call(
        arrange,
        out_shape=jax.ShapeDtypeStruct((shots, rcv, samples), bf16),
        in_specs=[vmem],
        out_specs=vmem,
        scratch_shapes=[
            tiled(rows, WIDTH),
            tiled(samples, rcv * shots),
            tiled(shots * rcv, samples),
        ],
    )(y)


def swap_groups(rows, size):
    lane = lax.broadcasted_iota(jnp.int32, rows[0].shape, 1) // size
    step = 1
    while step < len(rows):
        keep = (lane // step) % 2 == 0
        turned = list(rows)
        for i in range(len(rows)):
            if (i // step) % 2 == 0:
                a, b = rows[i], rows[i + step]
                turned[i] = jnp.where(keep, a, pltpu.roll(b, step * size, 1))
                turned[i + step] = jnp.where(keep, pltpu.roll(a, LANES - step * size, 1), b)
        rows = turned
        step *= 2
    return rows


def lag_response(response, lags, b_ref, y_ref, w_ref):
    shots, rows_e, taps = response.shape
    per_tile = LANES // rows_e
    b_ref[:, :taps] = response.reshape(shots * rows_e, taps)
    for tile in range(shots // per_tile):
        turned = b_ref[pl.ds(tile * LANES, LANES), :].T.astype(jnp.float32)
        y_ref[tile] = jnp.concatenate([turned[lags:taps], turned[:lags]])
        rows = [y_ref[tile, pl.ds(j, taps // lags, stride=lags), :] for j in range(lags)]
        for i, value in enumerate(swap_groups(rows, rows_e)):
            w_ref[pl.ds(tile * per_tile + i, taps // lags, stride=shots), :] = value
    return w_ref[...].astype(jnp.bfloat16)


def delayed(x, lag):
    if lag == 0:
        return x
    blank = jnp.zeros((x.shape[0], lag), x.dtype)
    return jnp.concatenate([blank, x[:, : x.shape[1] - lag]], axis=1)


def predict_line(
    n_shot, n_rcv, lags, chunks,
    response_hbm, traces_hbm, o_ref,
    response_ref, b_ref, y_ref, w_ref, gland, tland, a_ref, first_ref, second_ref, p_ref, part_ref, f_ref,
    load, sent, tmate, tpeer, tfar, gline, gside, gover, joined,
):
    shots, rows_e, taps = response_ref.shape
    rows_d, rcv, samples = tland.shape[1:]
    steps = taps // lags
    length = n_rcv // 2
    me_d, me_e = lax.axis_index("shot"), lax.axis_index("rcv")
    in_d, in_e = lax.rem(me_d, 2), lax.rem(me_e, 2)
    out_d, place = me_d // 2, me_e // 2
    mate_d = me_d + 1 - 2 * in_d
    mate_e = me_e + 1 - 2 * in_e
    peer_d = lax.rem(me_d + 2, n_shot)
    far_d = lax.rem(mate_d + 2, n_shot)
    low_bit, high_bit = lax.rem(place, 2), place // 2
    spots = [
        place + (n % 2) * (1 - 2 * low_bit) + (n // 2) * (2 - 4 * high_bit)
        for n in range(length)
    ]
    peers = [
        ((mate_d, me_e), in_d == 1, 0),
        ((peer_d, me_e), out_d == 1, 1),
        ((me_d, mate_e), in_e == 1, 2),
    ]
    peers += [((me_d, 2 * spots[n] + in_e), spots[n] < place, 2 + n) for n in range(1, length)]

    def hold(sem, count):
        @pl.when(count > 0)
        def _():
            pl.semaphore_wait(sem, count)

    barrier = pltpu.get_barrier_semaphore()
    for peer, below, _ in peers:
        @pl.when(jnp.logical_not(below))
        def _():
            pl.semaphore_signal(barrier, inc=1, device_id=peer, device_id_type=MESH)
    fetch_r = pltpu.make_async_copy(response_hbm, response_ref, load.at[0])
    fetch_t = pltpu.make_async_copy(traces_hbm, tland.at[me_d], load.at[1])
    share = shots // 4
    for i in range(4):
        some = pl.ds(i * share, share)
        pltpu.make_async_copy(response_hbm.at[some], response_ref.at[some], load.at[0]).start()
    fetch_t.start()
    with jax.named_scope("barrier"):
        hold(barrier, in_d + out_d + in_e + place)
    for peer, below, kind in peers:
        @pl.when(below)
        def _():
            pl.semaphore_signal(
                joined.at[kind], inc=1, device_id=peer, device_id_type=MESH
            )

    part = rows_d // chunks
    per_half = chunks // 2

    def tpiece(n):
        return pl.ds(lax.rem(n + in_e * per_half, chunks) * part, part)

    def tcopy(owner, n, recv, peer, src=None):
        piece = tpiece(n)
        return pltpu.make_async_remote_copy(
            src_ref=tland.at[owner, piece] if src is None else src.at[piece],
            dst_ref=tland.at[owner, piece],
            send_sem=sent.at[0],
            recv_sem=recv,
            device_id=peer,
            device_id_type=MESH,
        )

    cuts = 4
    cut = steps * shots // cuts

    def gcopy(owner, h, recv, peer):
        piece = gland.at[owner, pl.ds(h * cut, cut)]
        return pltpu.make_async_remote_copy(
            src_ref=piece,
            dst_ref=piece,
            send_sem=sent.at[1],
            recv_sem=recv,
            device_id=peer,
            device_id_type=MESH,
        )

    def whole(owner, recv):
        return pltpu.make_async_remote_copy(
            src_ref=gland.at[owner],
            dst_ref=gland.at[owner],
            send_sem=sent.at[1],
            recv_sem=recv,
            device_id=(me_d, mate_e),
            device_id_type=MESH,
        )

    across = [tcopy(me_d, n, tpeer.at[n], (peer_d, me_e), traces_hbm) for n in range(chunks)]
    beside = pltpu.make_async_remote_copy(
        src_ref=traces_hbm, dst_ref=tland.at[me_d], send_sem=sent.at[0], recv_sem=tmate.at[0],
        device_id=(mate_d, me_e), device_id_type=MESH,
    )
    side = [gcopy(me_e, h, gside.at[0], (me_d, mate_e)) for h in range(cuts)]
    along = []
    for spot in range(length):
        n = jnp.where(low_bit == spot % 2, 0, 1) + jnp.where(high_bit == spot // 2, 0, 2)
        n = jnp.maximum(n, 1)
        along.append([gcopy(me_e, h, gline.at[n - 1, h], (me_d, 2 * spot + in_e)) for h in range(cuts)])

    def launch(copies, when):
        @pl.when(when)
        def _():
            for copy in copies:
                copy.start()

    launch(across, out_d == 1)
    launch([beside], in_d == 1)
    with jax.named_scope("fetch_r"):
        fetch_r.wait()
    with jax.named_scope("turn_r"):
        gland[me_e] = lag_response(response_ref[...], lags, b_ref, y_ref, w_ref)
    launch(side, in_e == 1)
    launch(along[0], place > 0)
    with jax.named_scope("join_m"):
        hold(joined.at[0], 1 - in_d)
    launch([beside], in_d == 0)

    first_z = place == 0
    swap = jnp.where(place == 2, 1, 0)
    flip = jnp.where(jnp.logical_or(place == 3, jnp.logical_and(place == 1, in_d == 1)), 1, 0)
    in_turn = [1 + swap, 2 - swap + flip, 3 - flip]
    mixed = [
        (1, 0), (1, 1), (2, 0), (1, 2), (3, 0), (3, 1), (2, 1), (1, 3), (3, 2), (2, 2), (3, 3), (2, 3)
    ]
    late = jnp.logical_and(place == 1, in_d == 0)
    paired = [(1, h) for h in range(cuts)]
    paired += [(n, h) for part in range(2) for n in (2, 3) for h in (2 * part, 2 * part + 1)]
    turn = [
        (
            jnp.where(first_z, mixed[k][0], jnp.where(late, paired[k][0], in_turn[k // cuts])),
            jnp.where(first_z, mixed[k][1], jnp.where(late, paired[k][1], k % cuts)),
        )
        for k in range(3 * cuts)
    ]

    def spot_of(n):
        return sum(jnp.where(n == i, spots[i], 0) for i in range(length))

    def own(n):
        return 2 * spot_of(n) + in_e

    def other(n):
        return 2 * spot_of(n) + 1 - in_e

    def pass_r(k):
      with jax.named_scope(f"fr{k}"):
        n, h = turn[k]
        gcopy(own(n), h, gline.at[n - 1, h], (me_d, mate_e)).wait_recv()
        gcopy(own(n), h, gover.at[h // (cuts // 2)], (me_d, mate_e)).start()

    def pass_t(n):
      with jax.named_scope(f"ft{n}"):
        tcopy(peer_d, n, tpeer.at[n], (mate_d, me_e)).wait_recv()
        tcopy(peer_d, n, tfar.at[n // per_half], (mate_d, me_e)).start()

    def spreading(d, i):
        raw = tland[d, pl.ds(lax.rem(i + in_e, 2) * rows_e, rows_e)]
        put(a_ref, raw.astype(jnp.float32).reshape(rows_e * rcv, samples))
        out_ref = second_ref if i else first_ref

        def row(r):
            x = get_rows(a_ref, r, rows_e, rcv).astype(jnp.bfloat16)
            for j in range(lags):
                out_ref[d, r, pl.ds(j * rows_e, rows_e), :] = delayed(x, j)

        return row

    def spread(d, i):
        with jax.named_scope("spread"):
            row = spreading(d, i)
            for r in range(rcv):
                row(r)

    def far(i):
        with jax.named_scope("wfar"):
            landed = tland.at[far_d, pl.ds(lax.rem(i + in_e, 2) * rows_e, rows_e)]
            pltpu.make_async_copy(landed, landed, tfar.at[i]).wait()

    def meet(part):
      with jax.named_scope("meet"):
        if part == 0:
            whole(2 * place + 1 - in_e, gside.at[0]).wait_recv()
        rows = gland.at[pl.ds(0, length - 1), pl.ds(0, steps * shots // 2)]
        pltpu.make_async_copy(rows, rows, gover.at[part]).wait()

    def gather(rows, beside):
        with jax.named_scope("gather"):
            row = spreading(*beside)
            held = jnp.concatenate([gland[2 * z + in_e] for z in spots], axis=1)
            for n, r in enumerate(rows):
                p_ref[r] = jnp.dot(
                    held,
                    jnp.concatenate([first_ref[z, r] for z in spots], axis=0),
                    preferred_element_type=jnp.float32,
                )
                for i in range(n * rcv // len(rows), (n + 1) * rcv // len(rows)):
                    row(i)

    def close(part):
        with jax.named_scope("close"):
            count = steps // 2
            rows = pl.ds(part * count * shots, count * shots)
            held = jnp.concatenate([gland[2 * z + 1 - in_e, rows] for z in spots], axis=1)
            lane = lax.broadcasted_iota(jnp.int32, (shots, LANES), 1)
            for r in range(rcv):
                before = [0.0] * count
                for c in range(samples // WIDTH):
                    cols = pl.ds(c * WIDTH, WIDTH)
                    total = p_ref[r, rows, cols] + jnp.dot(
                        held,
                        jnp.concatenate([second_ref[z, r, :, cols] for z in spots], axis=0),
                        preferred_element_type=jnp.float32,
                    )
                    for t in range(WIDTH // LANES):
                        at = c * WIDTH // LANES + t
                        tile = pl.ds(at * LANES, LANES)
                        value = None if part == 0 else part_ref[r, :, tile]
                        for n in range(count):
                            lag = (part * count + n + 1) % steps * lags
                            x = total[n * shots : (n + 1) * shots, t * LANES : (t + 1) * LANES]
                            if lag > 0:
                                turned = pltpu.roll(x, lag, 1)
                                x = jnp.where(lane >= lag, turned, before[n])
                                before[n] = turned
                            value = x if value is None else value + x
                        if part == 0:
                            part_ref[r, :, tile] = value
                        else:
                            f_ref[at, pl.ds(r, shots, stride=rcv), :] = value

    with jax.named_scope("fetch_t"):
        fetch_t.wait()
    spread(me_d, 0)
    spread(me_d, 1)
    with jax.named_scope("join_x"):
        hold(joined.at[1], 1 - out_d)
        launch(across, out_d == 0)
    with jax.named_scope("join_y"):
        hold(joined.at[2], 1 - in_e)
        launch(side, in_e == 0)
    for spot in range(1, length):
        n = jnp.where(low_bit == spot % 2, 0, 1) + jnp.where(high_bit == spot // 2, 0, 2)
        with jax.named_scope("join_z"):
            hold(joined.at[2 + jnp.maximum(n, 1)], jnp.where(spot > place, 1, 0))
        launch(along[spot], spot > place)
    for spot in reversed(range(1, length)):
        launch(along[spot], spot < place)
    @pl.when(place == 0)
    def _():
        pass_r(0)

    with jax.named_scope("wmate"):
        pltpu.make_async_remote_copy(
            src_ref=traces_hbm, dst_ref=tland.at[mate_d], send_sem=sent.at[0], recv_sem=tmate.at[0],
            device_id=(mate_d, me_e), device_id_type=MESH,
        ).wait_recv()
    spread(mate_d, 0)
    spread(mate_d, 1)
    pass_t(0)
    @pl.when(place > 0)
    def _():
        pass_r(0)

    for k in range(1, 4):
        pass_r(k)
    pass_t(1)
    spread(peer_d, 0)
    for k in range(4, 9):
        pass_r(k)
    pass_t(2)
    for k in range(9, 12):
        pass_r(k)
    pass_t(3)
    far(0)
    spread(far_d, 0)
    gather(range(rcv // 2), (peer_d, 1))
    far(1)
    gather(range(rcv // 2, rcv), (far_d, 1))
    for part in range(2):
        meet(part)
        close(part)
    with jax.named_scope("out"):
        o_ref[...] = get(f_ref).reshape(shots, rcv, samples).astype(jnp.bfloat16)
    with jax.named_scope("wsend"):
        gone = tland.at[pl.ds(0, n_shot - 1)]
        pltpu.make_async_copy(gone, gone, sent.at[0]).wait()
        gone = gland.at[pl.ds(0, n_rcv - 1)]
        pltpu.make_async_copy(gone, gone, sent.at[1]).wait()


def shards(n_shot, n_rcv, response, traces):
    shots, rows_e, taps = response.shape
    rows_d, rcv, samples = traces.shape
    lags = LANES // rows_e
    fits = n_shot == 4 and n_rcv == 8 and rows_d == 2 * rows_e and lags * 8 == taps
    if not fits or shots * (taps // lags) % WIDTH != 0:
        return shards_general(n_shot, n_rcv, response, traces)
    steps = taps // lags
    chunks = 4
    f32, bf16 = jnp.float32, jnp.bfloat16

    def tiled(height, across):
        return pltpu.VMEM((across // LANES, height, LANES), f32)

    dma = pltpu.SemaphoreType.DMA
    vmem = pl.BlockSpec(memory_space=pltpu.VMEM)
    hbm = pl.BlockSpec(memory_space=pl.ANY)
    y = pl.pallas_call(
        functools.partial(predict_line, n_shot, n_rcv, lags, chunks),
        out_shape=pltpu.VMEM((shots, rcv, samples), bf16),
        in_specs=[hbm] * 2,
        out_specs=vmem,
        scratch_shapes=[
            pltpu.VMEM(response.shape, bf16),
            pltpu.VMEM((shots * rows_e, LANES), bf16),
            tiled(taps, shots * rows_e),
            pltpu.VMEM((steps * shots, LANES), f32),
            pltpu.VMEM((n_rcv, steps * shots, LANES), bf16),
            pltpu.VMEM((n_shot, rows_d, rcv, samples), bf16),
            tiled(rows_e * rcv, samples),
            pltpu.VMEM((n_shot, rcv, LANES, samples), bf16),
            pltpu.VMEM((n_shot, rcv, LANES, samples), bf16),
            pltpu.VMEM((rcv, steps * shots, samples), f32),
            pltpu.VMEM((rcv, shots, samples), f32),
            tiled(shots * rcv, samples),
            dma((2,)),
            dma((2,)),
            dma((1,)),
            dma((chunks,)),
            dma((2,)),
            dma((n_rcv // 2 - 1, 4)),
            dma((1,)),
            dma((2,)),
            pltpu.SemaphoreType.REGULAR((n_rcv // 2 + 2,)),
        ],
        compiler_params=pltpu.CompilerParams(collective_id=1, has_side_effects=True),
    )(response, traces)
    return y


def solution(mesh):
    placed = P("shot", "rcv", None)
    return jax.shard_map(
        functools.partial(shards, mesh.shape["shot"], mesh.shape["rcv"]),
        mesh=mesh, in_specs=(placed, placed), out_specs=placed, check_vma=False,
    )
```
